32 devices in a mesh: grp: 2 (over y), anim: 8 (over z, x), mark: 2 (over core).
Axes of the slice: x: 2, y: 2, z: 4, core: 2. Of those that a mesh axis runs over, the one named last changes fastest.
Arguments:
- noncore_geno: int32 [2048, 512], P(('grp', 'anim'), 'mark'), parts along dimension 0, may hold values from 0 to 2
- noncore_codes: int32 [5, 2048], P(None, ('grp', 'anim')), parts along dimension 1, may hold values from 0 to 32, as said below
- core_geno: int32 [8192, 512], P('anim', 'mark'), may hold values from 0 to 2
- core_codes: int32 [5, 8192], P(None, 'anim'), may hold values from 0 to 32, as said below
- breed_freqs: float32 [5, 512], P(None, 'mark'), may hold values from 0.05 to 0.95
- core_inverse: bfloat16 [8192, 8192], P(None, 'anim'), may hold values from -0.25 to 0.25
Outputs:
- kinship_entries: bfloat16 [2048, 8192], P(('grp', 'anim'), 'mark'), parts along dimension 0
- inverse_weighted_kinship: bfloat16 [2048, 8192], P(('grp', 'anim'), 'mark'), parts along dimension 0
The draws below stay inside these ranges and needn't reach their ends.
There are 2 independent parts, one for each index of `grp`. The reference program is written for one: setup_inputs(seed, part) draws one part's arguments, and reference() takes and returns one part's arrays. A program takes and returns all parts, laid end to end along the dimension named above; an argument that names none is the same for every part. Nothing has to cross between parts.
Inputs may be any that keep to these rules, and one draw needn't show every extreme that they name: `noncore_codes`: each animal's 5 codes sum to 32. `core_codes`: each animal's 5 codes sum to 32.
All inputs are finite; a program needn't handle non-finite values.
Results may differ from the reference program's by a relative error of at most 0.0055.
Values may be sent and summed in bfloat16 or wider, within the bound.
A program may use at most 64 MiB of HBM per device.

```python
import math
import jax
import jax.numpy as jnp
from jax import lax

BREEDS = 5
PROVEN_INDIVIDS = 8192
SLAB_MARKERS = 512
YOUNG_INDIVIDS = 1024
N_MARK = 2


def mixture_codes(key, count):
    cuts = jax.random.randint(key, (BREEDS - 1, count), 0, 33)
    cuts = jnp.sort(cuts, axis=0)
    edges = jnp.concatenate([jnp.zeros((1, count), jnp.int32), cuts.astype(jnp.int32), jnp.full((1, count), 32, jnp.int32)], 0)
    proportions = edges[1:] - edges[:-1]
    purebred = (jnp.arange(BREEDS)[:, None] == 0).astype(jnp.int32) * 32
    leading = jnp.arange(count)[None, :] == 0
    return jnp.where(leading, purebred, proportions).astype(jnp.int32)


def draw_noncore_codes(key, part):
    return mixture_codes(jax.random.fold_in(key, 11), YOUNG_INDIVIDS)


def draw_core_codes(key, part):
    return mixture_codes(jax.random.fold_in(key, 23), PROVEN_INDIVIDS)


def with_ends(array, own_key, least, top_value):
    spot = [jax.random.randint(jax.random.fold_in(own_key, axis), (), 0, length) for axis, length in enumerate(array.shape)]
    main_axis = array.shape.index(max(array.shape))
    beside = spot[:main_axis] + [(spot[main_axis] + 1) % array.shape[main_axis]] + spot[main_axis + 1:]
    return array.at[tuple(spot)].set(least).at[tuple(beside)].set(top_value)


def block_scale(stream_key, shape, pieces, smallest, high):
    def one(dim, shards_of):
        heights = jax.random.uniform(jax.random.fold_in(jax.random.fold_in(stream_key, 6), dim), (shards_of,), jnp.float32, smallest / len(pieces), high / len(pieces))
        return jnp.repeat(jnp.exp(heights), shape[dim] // shards_of).reshape((-1,) + (1,) * (len(shape) - dim - 1))

    gain = one(*pieces[0])
    for cut in pieces[1:]:
        gain = gain * one(*cut)
    return gain


def noise(key, dims, scale, limit, pieces=(), kind=jnp.bfloat16):
    result = jax.random.normal(key, dims, jnp.float32) * scale
    if len(pieces) > 0:
        result = block_scale(key, dims, pieces, -0.22, 0.18) * result
    return jnp.clip(result, min=-limit, max=limit).astype(kind)


def setup_inputs(seed: int = 0, part: int = 0) -> dict:
    seeds = jax.random.split(jax.random.key(seed), 7)
    own_keys = jax.random.split(jax.random.fold_in(seeds[6], part), 7)
    noncore_geno = with_ends(jax.random.randint(own_keys[0], (YOUNG_INDIVIDS, SLAB_MARKERS), 0, 3), jax.random.fold_in(own_keys[0], 1), 0, 2).astype(jnp.int32)
    noncore_codes = draw_noncore_codes(jax.random.fold_in(jax.random.fold_in(seeds[6], part), 71), part)
    core_geno = with_ends(jax.random.randint(seeds[2], (PROVEN_INDIVIDS, SLAB_MARKERS), 0, 3), jax.random.fold_in(seeds[2], 1), 0, 2).astype(jnp.int32)
    core_codes = draw_core_codes(jax.random.fold_in(seeds[6], 71), part)
    breed_freqs = jnp.clip(0.05 + 0.9 * jax.random.uniform(seeds[4], (BREEDS, SLAB_MARKERS), jnp.float32) ** block_scale(seeds[4], (BREEDS, SLAB_MARKERS), ((1, 2),), -0.2, 0.2), 0.05, 0.95)
    core_inverse = noise(seeds[5], (PROVEN_INDIVIDS, PROVEN_INDIVIDS), (PROVEN_INDIVIDS // 16) ** -0.5, 0.25, ((1, 8),))
    return {"noncore_geno": noncore_geno, "noncore_codes": noncore_codes, "core_geno": core_geno, "core_codes": core_codes, "breed_freqs": breed_freqs, "core_inverse": core_inverse}


def centre_value(genotypes, breed_codes, breed_freqs):
    fractions = breed_codes.astype(jnp.float32) / 32.0
    expected = lax.dot_general(fractions, breed_freqs, (((0,), (0,)), ((), ())), precision=lax.Precision.HIGHEST)
    return (genotypes.astype(jnp.float32) - 2.0 * expected).astype(jnp.bfloat16)


def reference(noncore_geno, noncore_codes, core_geno, core_codes, breed_freqs, core_inverse):
    noncore_z = centre_value(noncore_geno, noncore_codes, breed_freqs)
    core_z = centre_value(core_geno, core_codes, breed_freqs)
    half_marks = SLAB_MARKERS // N_MARK
    loadings = []
    for half_index in range(N_MARK):
        window = core_z[:, half_index * half_marks:(half_index + 1) * half_marks]
        loadings.append(jnp.dot(window.T, core_inverse, preferred_element_type=jnp.float32).astype(jnp.bfloat16))
    block_rows = math.gcd(YOUNG_INDIVIDS, 1024)
    number_of_tiles = noncore_z.reshape(YOUNG_INDIVIDS // block_rows, block_rows, SLAB_MARKERS)

    def kinship_submatrix(block_z):
        relate_total = jnp.zeros((block_rows, PROVEN_INDIVIDS), jnp.float32)
        regress_total = jnp.zeros((block_rows, PROVEN_INDIVIDS), jnp.float32)
        for half_index in range(N_MARK):
            low = half_index * half_marks
            part_z = block_z[:, low:low + half_marks]
            relate_part = jnp.dot(part_z, core_z[:, low:low + half_marks].T, preferred_element_type=jnp.float32) / SLAB_MARKERS
            regress_part = jnp.dot(part_z, loadings[half_index], preferred_element_type=jnp.float32) / SLAB_MARKERS
            relate_total = relate_total + lax.optimization_barrier(relate_part.astype(jnp.bfloat16)).astype(jnp.float32)
            regress_total = regress_total + lax.optimization_barrier(regress_part.astype(jnp.bfloat16)).astype(jnp.float32)
        return relate_total.astype(jnp.bfloat16), regress_total.astype(jnp.bfloat16)

    kinship_entries, inverse_weighted_kinship = lax.map(kinship_submatrix, number_of_tiles)
    return kinship_entries.reshape(YOUNG_INDIVIDS, PROVEN_INDIVIDS), inverse_weighted_kinship.reshape(YOUNG_INDIVIDS, PROVEN_INDIVIDS)
```

```python
import functools

import jax
import jax.numpy as jnp
from jax import lax
from jax.experimental import pallas as pl
from jax.experimental.pallas import tpu as pltpu
from jax.sharding import PartitionSpec as P

MESH = pl.DeviceIdType.MESH
F32 = jnp.float32
BF16 = jnp.bfloat16


def centre_value(genotypes, breed_codes, breed_freqs):
    fractions = breed_codes.astype(F32) / 32.0
    expected = lax.dot_general(
        fractions, breed_freqs, (((0,), (0,)), ((), ())), precision=lax.Precision.HIGHEST
    )
    return (genotypes.astype(F32) - 2.0 * expected).astype(BF16)


def plain_body(markers, noncore_geno, noncore_codes, core_geno, core_codes, breed_freqs, core_inverse):
    noncore_z = centre_value(noncore_geno, noncore_codes, breed_freqs)
    core_z = centre_value(core_geno, core_codes, breed_freqs)
    rows = lax.all_gather(core_z, "anim", axis=0, tiled=True)
    related = (
        lax.dot_general(noncore_z, rows, (((1,), (1,)), ((), ())), preferred_element_type=F32) / markers
    )
    loading = lax.dot_general(rows, core_inverse, (((0,), (0,)), ((), ())), preferred_element_type=F32)
    scores = (
        jnp.dot(
            noncore_z,
            lax.all_gather(loading.astype(BF16), "anim", axis=1, tiled=True),
            preferred_element_type=F32,
        )
        / markers
    )
    return tuple(
        lax.psum_scatter(v.astype(BF16), "mark", scatter_dimension=1, tiled=True) for v in (related, scores)
    )


def kernel(
    n, nc, scale, geno_hbm, codes_hbm, freqs_hbm, ngeno_hbm, ncodes_hbm, inv_hbm, kin_out, reg_out,
    RAW, codes, freqs, ngeno, ncodes, TF, TC, G, H, INV, ACC, NF, NO, NB, LF, PO, PR, KO, R,
    raw_sem, in_sem, inv_sem, g_recv, up_send, dn_send, x_send, h_send, h_recv,
    n_send, n_recv, nb_loc, nb_zsend, nb_xsend, nb_recv, l_send, l_recv,
    p_send, p_recv, r_send, r_recv, r_loc,
):
    nz, nh = n // 2, n // 2
    y, a, m = lax.axis_index("grp"), lax.axis_index("anim"), lax.axis_index("mark")
    z, x = a // 2, lax.rem(a, 2)
    o = 1 - m
    q, cols = G.shape[1:]
    breeds = freqs.shape[0]
    cw = cols // nc
    own_half = a // nh
    here = pl.ds(pl.multiple_of(y * q, q), q)
    there = pl.ds(pl.multiple_of((1 - y) * q, q), q)

    def remote(src, dst, ss, rs, g=None, an=None, mk=None):
        return pltpu.make_async_remote_copy(
            src_ref=src, dst_ref=dst, send_sem=ss, recv_sem=rs,
            device_id=(y if g is None else g, a if an is None else an, m if mk is None else mk),
            device_id_type=MESH,
        )

    def inv_copy(b):
        return pltpu.make_async_copy(inv_hbm.at[pl.ds(b * cols, cols)], INV.at[b], inv_sem.at[b])

    raw = pltpu.make_async_copy(geno_hbm.at[:, here], RAW, raw_sem)
    small = [
        pltpu.make_async_copy(src, dst, in_sem.at[i])
        for i, (src, dst) in enumerate(
            ((codes_hbm, codes), (freqs_hbm, freqs), (ngeno_hbm, ngeno), (ncodes_hbm, ncodes))
        )
    ]
    raw.start()
    for copy in small:
        copy.start()

    barrier = pltpu.get_barrier_semaphore()

    def greet(i, c):
        an, mk = i // 2, lax.rem(i, 2)

        @pl.when((an != a) | (mk != m))
        def _():
            pl.semaphore_signal(barrier, inc=1, device_id=(y, an, mk), device_id_type=MESH)

        return c

    lax.fori_loop(0, 2 * n, greet, 0)
    pl.semaphore_signal(barrier, inc=1, device_id=(1 - y, a, m), device_id_type=MESH)

    TF[...] = jnp.zeros_like(TF)
    TC[...] = jnp.zeros_like(TC)
    for copy in small:
        copy.wait()
    TF[:breeds, :] = freqs[:, here]
    TC[:breeds, :] = ncodes[...].astype(F32) / 32.0
    freq_t = TF[...].T
    code_t = TC[...].T
    expected = code_t[:, 0:1] * freqs[0:1, :]
    for b in range(1, breeds):
        expected += code_t[:, b : b + 1] * freqs[b : b + 1, :]
    NF[m] = (ngeno[...].astype(F32) - 2.0 * expected).astype(BF16)
    raw.wait()
    lax.fori_loop(0, n, lambda i, c: (inv_copy(lax.rem(a + i, n)).start(), c)[1], 0)
    for t in range(0, cols, 128):
        span = slice(t, t + 128)
        expected = freq_t[:, 0:1] * (codes[0:1, span].astype(F32) / 32.0)
        for b in range(1, breeds):
            expected += freq_t[:, b : b + 1] * (codes[b : b + 1, span].astype(F32) / 32.0)
        G[a, :, span] = (RAW[span, :].astype(F32).T - 2.0 * expected).astype(BF16)
    ACC[...] = jnp.zeros_like(ACC)
    pl.semaphore_wait(barrier, 2 * n)

    half_q = q // 2

    def piece(b, p):
        return G.at[b, pl.ds(pl.multiple_of(p * half_q, half_q), half_q)]

    def go_up(b, p):
        return remote(piece(b, p), piece(b, p), up_send.at[b, p], g_recv.at[b, p], an=a + 2)

    def go_dn(b, p):
        return remote(piece(b, p), piece(b, p), dn_send.at[b, p], g_recv.at[b, p], an=a - 2)

    def go_x(b, p):
        return remote(piece(b, p), piece(b, p), x_send.at[b, p], g_recv.at[b, p], an=a + 1 - 2 * x)

    def go_partner(b):
        i = lax.rem(b, nh)
        return remote(G.at[b], H.at[i], h_send.at[i], h_recv.at[i], mk=o)

    npart = remote(NF.at[m], NF.at[m], n_send.at[0], n_recv.at[0], mk=o)
    npart.start()

    for p in range(2):

        @pl.when(z < nz - 1)
        def _():
            go_up(a, p).start()

        @pl.when(z > 0)
        def _():
            go_dn(a, p).start()

        go_x(a, p).start()

    npart.wait_send()
    remote(NF.at[o], NF.at[o], n_send.at[0], n_recv.at[0], mk=o).wait_recv()
    nother = remote(NF, NO, n_send.at[1], n_recv.at[1], g=1 - y)
    nother.start()

    def nb_z(i):
        return remote(NF, NB.at[z], nb_zsend.at[i], nb_recv.at[z], an=2 * i + x)

    def nb_x(src, i):
        return remote(src, NB.at[i], nb_xsend.at[i], nb_recv.at[i], an=a + 1 - 2 * x)

    nb_local = pltpu.make_async_copy(NF, NB.at[z], nb_loc)

    @pl.when(m == x)
    def _():
        nb_local.start()

    def p_copy(i):
        return remote(PO.at[i], PR.at[i], p_send.at[i], p_recv.at[i], g=1 - y)

    def relate(i):
        b = m * nh + i
        go_partner(b).wait_recv()
        mine, his = G[b], H[i]

        def both(ref):
            return (
                jnp.dot(ref[m, :, here], mine, preferred_element_type=F32)
                + jnp.dot(ref[o, :, here], his, preferred_element_type=F32)
            ) * scale

        PO[i] = both(NO).astype(BF16)
        p_copy(i).start()
        KO[i] = both(NF)

    late = nz - 1

    def is_late(b):
        d = jnp.abs(b // 2 - z) + jnp.where(lax.rem(b, 2) == x, 0, 1)
        return d >= late

    def step(s, c):
        def hop(k, c):
            j, p = lax.rem(k, 2), k // 2
            zz = z + s * (2 * j - 1)

            @pl.when((s > 0) & (zz >= 0) & (zz < nz))
            def _():
                b = 2 * zz + x
                go_up(b, p).wait_recv()

                @pl.when((j == 0) & (z < nz - 1))
                def _():
                    go_up(b, p).start()

                @pl.when((j == 1) & (z > 0))
                def _():
                    go_dn(b, p).start()

                go_x(b, p).start()

            return c

        lax.fori_loop(0, 4, hop, 0)

        @pl.when((s == late) & (m == x))
        def _():
            def send(i, c):
                @pl.when(i != z)
                def _():
                    nb_z(i).start()

                return c

            lax.fori_loop(0, nz, send, 0)
            nb_x(NF, z).start()

        def use(k, c):
            j, side = lax.rem(k, 2), k // 2
            d = s - side
            zz = z + d * (2 * j - 1)

            @pl.when((d >= 0) & (zz >= 0) & (zz < nz) & ((d > 0) | (j == 0)))
            def _():
                b = 2 * zz + x + side * (1 - 2 * x)

                @pl.when(side == 1)
                def _():
                    go_x(b, 0).wait_recv()
                    go_x(b, 1).wait_recv()

                @pl.when(b // nh == o)
                def _():
                    go_partner(b).start()

                inv_copy(b).wait()
                left = G[b]
                width = 256 if cols % 256 == 0 else 128
                for t in range(0, cols, width):
                    ACC[:, t : t + width] += jnp.dot(
                        left, INV[b, :, t : t + width], preferred_element_type=F32
                    )

                @pl.when((b // nh == m) & (s < late))
                def _():
                    @pl.when(s == 0)
                    def _():
                        nother.wait_recv()

                    relate(lax.rem(b, nh))

            return c

        lax.fori_loop(0, 4, use, 0)

        @pl.when((s == 0) & (own_half != m))
        def _():
            nother.wait_recv()

        return c

    lax.fori_loop(0, nz + 1, step, 0)

    def l_y(c):
        return remote(LF.at[c, m, here], LF.at[c, m, here], l_send.at[0, c], l_recv.at[0, c], g=1 - y)

    def l_p(c):
        return remote(LF.at[c, m, here], LF.at[c, m, here], l_send.at[1, c], l_recv.at[1, c], mk=o)

    def l_f(c):
        return remote(LF.at[c, m, there], LF.at[c, m, there], l_send.at[2, c], l_recv.at[2, c], mk=o)

    for c in range(nc):
        LF[c, m, here, :] = ACC[:, c * cw : (c + 1) * cw].astype(BF16)
        l_y(c).start()
        l_p(c).start()

    @pl.when(m == x)
    def _():
        def pass_on(i, c):
            @pl.when(i != z)
            def _():
                nb_z(i).wait_send()
                nb_x(NB.at[i], i).wait_recv()
                nb_x(NB.at[i], i).start()

            return c

        lax.fori_loop(0, nz, pass_on, 0)
        nb_local.wait()

    @pl.when(m != x)
    def _():
        lax.fori_loop(0, nz, lambda i, c: (nb_x(NB.at[i], i).wait_recv(), c)[1], 0)

    def window(b, c):
        return pl.ds(pl.multiple_of(lax.rem(b, nh) * cols + c * cw, cw), cw)

    def r_copy(i, c):
        return remote(
            R.at[c, i], reg_out.at[:, window(a, c)], r_send.at[c, i], r_recv.at[c, lax.rem(a, nh)],
            an=2 * i + m, mk=own_half,
        )

    def r_local(c):
        return pltpu.make_async_copy(R.at[c, z], reg_out.at[:, window(a, c)], r_loc.at[c])

    keep = (m == x) & (own_half == m)

    def chunk(c, carry):
        @pl.when(c < nc)
        def _():
            l_y(c).wait_recv()
            l_f(c).start()

        @pl.when(c > 0)
        def _():
            e = c - 1
            l_p(e).wait_recv()
            l_f(e).wait_recv()

            def regress(i, carry):
                zz = lax.rem(z + nz // 2 + i, nz)
                R[e, zz] = (
                    (
                        jnp.dot(NB[zz, 0], LF[e, 0], preferred_element_type=F32)
                        + jnp.dot(NB[zz, 1], LF[e, 1], preferred_element_type=F32)
                    )
                    * scale
                ).astype(BF16)

                @pl.when((zz == z) & keep)
                def _():
                    r_local(e).start()

                @pl.when((zz != z) | jnp.logical_not(keep))
                def _():
                    r_copy(zz, e).start()

                return carry

            lax.fori_loop(0, nz, regress, 0)

        return carry

    lax.fori_loop(0, nc + 1, chunk, 0)

    def rest(i, c):
        @pl.when(is_late(m * nh + i))
        def _():
            relate(i)

        return c

    lax.fori_loop(0, nh, rest, 0)
    nother.wait_send()
    for i in range(nh):
        p_copy(i).wait_recv()
        kin_out[:, i * cols : (i + 1) * cols] = (KO[i] + PR[i].astype(F32)).astype(BF16)

    def l_sends(c, carry):
        l_y(c).wait_send()
        l_p(c).wait_send()
        l_f(c).wait_send()

        @pl.when(keep)
        def _():
            r_local(c).wait()

        def r_sends(i, carry):
            @pl.when((i != z) | jnp.logical_not(keep))
            def _():
                r_copy(i, c).wait_send()

            return carry

        lax.fori_loop(0, nz, r_sends, 0)

        def r_recvs(i, carry):
            b = m * nh + i

            @pl.when((b != a) | jnp.logical_not(keep))
            def _():
                remote(
                    R.at[c, 0], reg_out.at[:, window(i, c)], r_send.at[c, 0], r_recv.at[c, i], mk=o
                ).wait_recv()

            return carry

        lax.fori_loop(0, nh, r_recvs, 0)
        return carry

    lax.fori_loop(0, nc, l_sends, 0)
    lax.fori_loop(0, nh, lambda i, c: (p_copy(i).wait_send(), c)[1], 0)

    def g_sends(b, c):
        zz = b // 2

        @pl.when(lax.rem(b, 2) == x)
        def _():
            for p in range(2):
                go_x(b, p).wait_send()

                @pl.when((zz <= z) & (z < nz - 1))
                def _():
                    go_up(b, p).wait_send()

                @pl.when((zz >= z) & (z > 0))
                def _():
                    go_dn(b, p).wait_send()

        @pl.when(b // nh == o)
        def _():
            go_partner(b).wait_send()

        return c

    lax.fori_loop(0, n, g_sends, 0)

    @pl.when(m == x)
    def _():
        lax.fori_loop(0, nz, lambda i, c: (nb_x(NF, i).wait_send(), c)[1], 0)


def store_kernel(kin_ref, reg_ref, kin_out, reg_out, sem):
    copies = [
        pltpu.make_async_copy(src, dst, sem.at[i])
        for i, (src, dst) in enumerate(((kin_ref, kin_out), (reg_ref, reg_out)))
    ]
    for copy in copies:
        copy.start()
    for copy in copies:
        copy.wait()


def kernel_body(n, markers, noncore_geno, noncore_codes, core_geno, core_codes, breed_freqs, core_inverse):
    half = core_geno.shape[1]
    q = half // 2
    cols = core_inverse.shape[1]
    rows = noncore_geno.shape[0]
    nh = nz = n // 2
    nc = 4 if cols % 512 == 0 else 1
    cw = cols // nc
    vmem = pl.BlockSpec(memory_space=pltpu.VMEM)
    anyspace = pl.BlockSpec(memory_space=pl.ANY)
    hbm = pl.BlockSpec(memory_space=pltpu.HBM)
    D = pltpu.SemaphoreType.DMA
    out = jax.ShapeDtypeStruct((rows, nh * cols), BF16)
    held = pltpu.VMEM((rows, nh * cols), BF16)
    related, scores = pl.pallas_call(
        functools.partial(kernel, n, nc, 1.0 / markers),
        out_shape=(held, held),
        in_specs=[hbm] * 6,
        out_specs=(vmem, vmem),
        scratch_shapes=[
            pltpu.VMEM((cols, q), jnp.int32),
            pltpu.VMEM(core_codes.shape, jnp.int32),
            pltpu.VMEM(breed_freqs.shape, F32),
            pltpu.VMEM(noncore_geno.shape, jnp.int32),
            pltpu.VMEM(noncore_codes.shape, jnp.int32),
            pltpu.VMEM((128, q), F32),
            pltpu.VMEM((128, rows), F32),
            pltpu.VMEM((n, q, cols), BF16),
            pltpu.VMEM((nh, q, cols), BF16),
            pltpu.VMEM((n, cols, cols), BF16),
            pltpu.VMEM((q, cols), F32),
            pltpu.VMEM((2, rows, half), BF16),
            pltpu.VMEM((2, rows, half), BF16),
            pltpu.VMEM((nz, 2, rows, half), BF16),
            pltpu.VMEM((nc, 2, half, cw), BF16),
            pltpu.VMEM((nh, rows, cols), BF16),
            pltpu.VMEM((nh, rows, cols), BF16),
            pltpu.VMEM((nh, rows, cols), F32),
            pltpu.VMEM((nc, nz, rows, cw), BF16),
            D, D((4,)), D((n,)), D((n, 2)), D((n, 2)), D((n, 2)), D((n, 2)), D((nh,)), D((nh,)),
            D((2,)), D((2,)), D, D((nz,)), D((nz,)), D((nz,)), D((3, nc)), D((3, nc)),
            D((nh,)), D((nh,)), D((nc, nz)), D((nc, nh)), D((nc,)),
        ],
        compiler_params=pltpu.CompilerParams(
            collective_id=0, has_side_effects=True, vmem_limit_bytes=54 * 1024 * 1024
        ),
    )(core_geno, core_codes, breed_freqs, noncore_geno, noncore_codes, core_inverse)
    return pl.pallas_call(
        store_kernel,
        out_shape=(out, out),
        in_specs=[vmem] * 2,
        out_specs=(anyspace, anyspace),
        scratch_shapes=[D((2,))],
    )(*(pltpu.with_memory_space_constraint(v, pltpu.VMEM) for v in (related, scores)))


def solution(mesh):
    in_specs = (
        P(("grp", "anim"), "mark"),
        P(None, ("grp", "anim")),
        P("anim", "mark"),
        P(None, "anim"),
        P(None, "mark"),
        P(None, "anim"),
    )
    out_specs = (P(("grp", "anim"), "mark"), P(("grp", "anim"), "mark"))
    n = mesh.shape["anim"]

    def body(*args):
        half, cols, rows = args[2].shape[1], args[5].shape[1], args[0].shape[0]
        markers = half * mesh.shape["mark"]
        fits = (
            mesh.shape["grp"] == 2 and mesh.shape["mark"] == 2 and n % 4 == 0
            and half % 256 == 0 and cols % 128 == 0 and rows % 128 == 0 and args[4].shape[0] <= 128
            and args[2].shape[0] == cols and n * cols * cols * 2 <= 24 * 2**20
        )
        if fits:
            return kernel_body(n, markers, *args)
        return plain_body(markers, *args)

    return jax.shard_map(body, mesh=mesh, in_specs=in_specs, out_specs=out_specs, check_vma=False)
```

```python
import functools

import jax
import jax.numpy as jnp
from jax import lax
from jax.experimental import pallas as pl
from jax.experimental.pallas import tpu as pltpu
from jax.sharding import PartitionSpec as P

MESH = pl.DeviceIdType.MESH
F32 = jnp.float32
BF16 = jnp.bfloat16


def centre_value(genotypes, breed_codes, breed_freqs):
    fractions = breed_codes.astype(F32) / 32.0
    expected = lax.dot_general(
        fractions, breed_freqs, (((0,), (0,)), ((), ())), precision=lax.Precision.HIGHEST
    )
    return (genotypes.astype(F32) - 2.0 * expected).astype(BF16)


def plain_body(markers, noncore_geno, noncore_codes, core_geno, core_codes, breed_freqs, core_inverse):
    noncore_z = centre_value(noncore_geno, noncore_codes, breed_freqs)
    core_z = centre_value(core_geno, core_codes, breed_freqs)
    rows = lax.all_gather(core_z, "anim", axis=0, tiled=True)
    related = (
        lax.dot_general(noncore_z, rows, (((1,), (1,)), ((), ())), preferred_element_type=F32) / markers
    )
    loading = lax.dot_general(rows, core_inverse, (((0,), (0,)), ((), ())), preferred_element_type=F32)
    scores = (
        jnp.dot(
            noncore_z,
            lax.all_gather(loading.astype(BF16), "anim", axis=1, tiled=True),
            preferred_element_type=F32,
        )
        / markers
    )
    return tuple(
        lax.psum_scatter(v.astype(BF16), "mark", scatter_dimension=1, tiled=True) for v in (related, scores)
    )


def kernel(
    n, nc, scale, geno_hbm, codes_hbm, freqs_hbm, ngeno_hbm, ncodes_hbm, inv_hbm, kin_out, reg_out,
    RAW, codes, freqs, ngeno, ncodes, TF, TC, G, H, INV, ACC, NF, NO, NB, LF, LM, PO, PR, KO, R,
    raw_sem, in_sem, inv_sem, g_recv, up_send, dn_send, x_send, h_send, h_recv,
    n_send, n_recv, nb_loc, nb_zsend, nb_xsend, nb_recv, l_send, l_recv, m_send, m_recv,
    p_send, p_recv, r_send, r_recv, r_loc,
):
    nz, nh = n // 2, n // 2
    y, a, m = lax.axis_index("grp"), lax.axis_index("anim"), lax.axis_index("mark")
    z, x = a // 2, lax.rem(a, 2)
    o = 1 - m
    q, hc = G.shape[2:]
    cols = 2 * hc
    breeds = freqs.shape[0]
    cw = cols // nc
    here = pl.ds(pl.multiple_of(y * q, q), q)
    there = pl.ds(pl.multiple_of((1 - y) * q, q), q)
    low = z < nz // 2
    mid = (z > 0) & (z < nz - 1)
    across = 2 * (nz - 1 - z) + x

    def is_end(zz):
        return (zz == 0) | (zz == nz - 1)

    def remote(src, dst, ss, rs, g=None, an=None, mk=None):
        return pltpu.make_async_remote_copy(
            src_ref=src, dst_ref=dst, send_sem=ss, recv_sem=rs,
            device_id=(y if g is None else g, a if an is None else an, m if mk is None else mk),
            device_id_type=MESH,
        )

    def inv_copy(b):
        return pltpu.make_async_copy(inv_hbm.at[pl.ds(b * cols, cols)], INV.at[b], inv_sem.at[b])

    raw = [
        pltpu.make_async_copy(geno_hbm.at[pl.ds(p * hc, hc), here], RAW.at[pl.ds(p * hc, hc)], raw_sem.at[p])
        for p in range(2)
    ]
    small = [
        pltpu.make_async_copy(src, dst, in_sem.at[i])
        for i, (src, dst) in enumerate(
            ((codes_hbm, codes), (freqs_hbm, freqs), (ngeno_hbm, ngeno), (ncodes_hbm, ncodes))
        )
    ]
    for copy in raw + small:
        copy.start()

    barrier = pltpu.get_barrier_semaphore()

    def greet(g=None, an=None, mk=None):
        pl.semaphore_signal(
            barrier, inc=1,
            device_id=(y if g is None else g, a if an is None else an, m if mk is None else mk),
            device_id_type=MESH,
        )

    greet(mk=o)
    greet(an=a + 1 - 2 * x)
    greet(g=1 - y)

    @pl.when(z < nz - 1)
    def _():
        greet(an=a + 2)

    @pl.when(z > 0)
    def _():
        greet(an=a - 2)

    lax.fori_loop(0, n, lambda i, c: (inv_copy(lax.rem(a + i, n)).start(), c)[1], 0)

    def go_up(b, p):
        return remote(G.at[b, p], G.at[b, p], up_send.at[b, p], g_recv.at[b, p], an=a + 2)

    def go_dn(b, p):
        return remote(G.at[b, p], G.at[b, p], dn_send.at[b, p], g_recv.at[b, p], an=a - 2)

    def go_x(b, p):
        return remote(G.at[b, p], G.at[b, p], x_send.at[b, p], g_recv.at[b, p], an=a + 1 - 2 * x)

    def go_partner(b):
        i = lax.rem(b, nh)
        return remote(G.at[b], H.at[i], h_send.at[i], h_recv.at[i], mk=o)

    TF[...] = jnp.zeros_like(TF)
    TC[...] = jnp.zeros_like(TC)
    small[0].wait()
    small[1].wait()
    TF[:breeds, :] = freqs[:, here]
    freq_t = TF[...].T
    for p in range(2):
        raw[p].wait()
        for t in range(0, hc, 128):
            at = slice(p * hc + t, p * hc + t + 128)
            expected = freq_t[:, 0:1] * (codes[0:1, at].astype(F32) / 32.0)
            for b in range(1, breeds):
                expected += freq_t[:, b : b + 1] * (codes[b : b + 1, at].astype(F32) / 32.0)
            G[a, p, :, t : t + 128] = (RAW[at, :].astype(F32).T - 2.0 * expected).astype(BF16)
        if p == 0:
            pl.semaphore_wait(barrier, 5 - jnp.where(mid, 0, 1))

        @pl.when(z < nz - 1)
        def _():
            go_up(a, p).start()

        @pl.when(z > 0)
        def _():
            go_dn(a, p).start()

        go_x(a, p).start()

    small[2].wait()
    small[3].wait()
    TC[:breeds, :] = ncodes[...].astype(F32) / 32.0
    code_t = TC[...].T
    expected = code_t[:, 0:1] * freqs[0:1, :]
    for b in range(1, breeds):
        expected += code_t[:, b : b + 1] * freqs[b : b + 1, :]
    NF[m] = (ngeno[...].astype(F32) - 2.0 * expected).astype(BF16)
    npart = remote(NF.at[m], NF.at[m], n_send.at[0], n_recv.at[0], mk=o)
    npart.start()
    ACC[...] = jnp.zeros_like(ACC)
    npart.wait_send()
    remote(NF.at[o], NF.at[o], n_send.at[0], n_recv.at[0], mk=o).wait_recv()
    nother = remote(NF, NO, n_send.at[1], n_recv.at[1], g=1 - y)
    nother.start()

    def wants(i, j):
        return is_end(i) | (i // (nz // 2) == j // (nz // 2))

    def nb_z(i):
        return remote(NF, NB.at[z], nb_zsend.at[i], nb_recv.at[z], an=2 * i + x)

    def nb_x(src, i):
        return remote(src, NB.at[i], nb_xsend.at[i], nb_recv.at[i], an=a + 1 - 2 * x)

    nb_local = pltpu.make_async_copy(NF, NB.at[z], nb_loc)

    @pl.when(m == x)
    def _():
        nb_local.start()

    def p_copy(i):
        return remote(PO.at[i], PR.at[i], p_send.at[i], p_recv.at[i], g=1 - y)

    def relate(i):
        go_partner(m * nh + i).wait_recv()
        for p in range(2):
            mine, his = G[m * nh + i, p], H[i, p]
            span = slice(p * hc, (p + 1) * hc)

            def both(ref):
                return (
                    jnp.dot(ref[m, :, here], mine, preferred_element_type=F32)
                    + jnp.dot(ref[o, :, here], his, preferred_element_type=F32)
                ) * scale

            PO[i, :, span] = both(NO).astype(BF16)
            KO[i, :, span] = both(NF)
        p_copy(i).start()

    late = nz - 1

    def is_late(b):
        d = jnp.abs(b // 2 - z) + jnp.where(lax.rem(b, 2) == x, 0, 1)
        return d >= late

    def step(s, c):
        def lift(j, c):
            zz = z + (s - 1) * (2 * j - 1)

            @pl.when((s > 0) & (zz == j * (nz - 1)))
            def _():
                b = 2 * zz + 1 - x
                go_x(b, 0).wait_recv()

                @pl.when((j == 0) & (z < nz - 1))
                def _():
                    go_up(b, 0).start()

                @pl.when((j == 1) & (z > 0))
                def _():
                    go_dn(b, 0).start()

            return c

        lax.fori_loop(0, 2, lift, 0)

        def hop(k, c):
            j, p = lax.rem(k, 2), k // 2
            zz = z + s * (2 * j - 1)

            @pl.when((s > 0) & (zz >= 0) & (zz < nz))
            def _():
                b = 2 * zz + x
                go_up(b, p).wait_recv()

                @pl.when((j == 0) & (z < nz - 1))
                def _():
                    go_up(b, p).start()

                @pl.when((j == 1) & (z > 0))
                def _():
                    go_dn(b, p).start()

                @pl.when((p > 0) | jnp.logical_not(is_end(zz)))
                def _():
                    go_x(b, p).start()

            return c

        lax.fori_loop(0, 4, hop, 0)

        @pl.when((s == late) & (m == x))
        def _():
            def send(i, c):
                @pl.when((i != z) & wants(i, z))
                def _():
                    nb_z(i).start()

                return c

            lax.fori_loop(0, nz, send, 0)
            nb_x(NF, z).start()

        def use(k, c):
            j, side = lax.rem(k, 2), k // 2
            d = s - side
            zz = z + d * (2 * j - 1)

            @pl.when((d >= 0) & (zz >= 0) & (zz < nz) & ((d > 0) | (j == 0)))
            def _():
                b = 2 * zz + x + side * (1 - 2 * x)

                @pl.when(side == 1)
                def _():
                    @pl.when(jnp.logical_not(is_end(zz)))
                    def _():
                        go_x(b, 0).wait_recv()

                    go_x(b, 1).wait_recv()

                @pl.when(b // nh == o)
                def _():
                    go_partner(b).start()

                inv_copy(b).wait()
                first, second = G[b, 0], G[b, 1]
                width = 256 if cols % 256 == 0 else 128
                for t in range(0, cols, width):
                    ACC[:, t : t + width] += jnp.dot(
                        first, INV[b, :hc, t : t + width], preferred_element_type=F32
                    ) + jnp.dot(second, INV[b, hc:, t : t + width], preferred_element_type=F32)

                @pl.when((b // nh == m) & (s < late))
                def _():
                    @pl.when(s == 0)
                    def _():
                        nother.wait_recv()

                    relate(lax.rem(b, nh))

            return c

        lax.fori_loop(0, 4, use, 0)

        @pl.when((s == 0) & (a // nh != m))
        def _():
            nother.wait_recv()

        return c

    lax.fori_loop(0, nz + 1, step, 0)

    def l_y(c):
        return remote(LF.at[c, m, here], LF.at[c, m, here], l_send.at[0, c], l_recv.at[0, c], g=1 - y)

    def l_p(c):
        return remote(LF.at[c, m, here], LF.at[c, m, here], l_send.at[1, c], l_recv.at[1, c], mk=o)

    def l_f(c):
        return remote(LF.at[c, m, there], LF.at[c, m, there], l_send.at[2, c], l_recv.at[2, c], mk=o)

    def m_z(c):
        return remote(LF.at[c, m, here], LM.at[c, m, here], m_send.at[3, c], m_recv.at[3, c], an=across)

    def m_y(c):
        return remote(LM.at[c, m, here], LM.at[c, m, here], m_send.at[0, c], m_recv.at[0, c], g=1 - y)

    def m_p(c):
        return remote(LM.at[c, m, here], LM.at[c, m, here], m_send.at[1, c], m_recv.at[1, c], mk=o)

    def m_f(c):
        return remote(LM.at[c, m, there], LM.at[c, m, there], m_send.at[2, c], m_recv.at[2, c], mk=o)

    for c in range(nc):
        LF[c, m, here, :] = ACC[:, c * cw : (c + 1) * cw].astype(BF16)

        @pl.when(mid)
        def _():
            m_z(c).start()

        l_y(c).start()
        l_p(c).start()

    @pl.when(m == x)
    def _():
        def pass_on(i, c):
            @pl.when((i != z) & wants(i, z))
            def _():
                nb_z(i).wait_send()

            @pl.when((i != z) & wants(z, i))
            def _():
                nb_x(NB.at[i], i).wait_recv()
                nb_x(NB.at[i], i).start()

            return c

        lax.fori_loop(0, nz, pass_on, 0)
        nb_local.wait()

    @pl.when(m != x)
    def _():
        def arrive(i, c):
            @pl.when(wants(z, i))
            def _():
                nb_x(NB.at[i], i).wait_recv()

            return c

        lax.fori_loop(0, nz, arrive, 0)

    def window(b, c):
        return pl.ds(pl.multiple_of(lax.rem(b, nh) * cols + c * cw, cw), cw)

    def r_copy(c, slot, zz, b):
        return remote(
            R.at[c, slot], reg_out.at[:, window(b, c)], r_send.at[c, slot], r_recv.at[c, lax.rem(b, nh)],
            an=2 * zz + m, mk=b // nh,
        )

    def r_local(c, slot, b):
        return pltpu.make_async_copy(R.at[c, slot], reg_out.at[:, window(b, c)], r_loc.at[c])

    keep = (m == x) & (a // nh == m)
    keep_across = mid & (m == x) & (across // nh == m)

    def product(c, slot, zz, b, ref, stays):
        R[c, slot] = (
            (
                jnp.dot(NB[zz, 0], ref[c, 0], preferred_element_type=F32)
                + jnp.dot(NB[zz, 1], ref[c, 1], preferred_element_type=F32)
            )
            * scale
        ).astype(BF16)

        @pl.when((zz == z) & stays)
        def _():
            r_local(c, slot, b).start()

        @pl.when((zz != z) | jnp.logical_not(stays))
        def _():
            r_copy(c, slot, zz, b).start()

    def near(i):
        return jnp.where(low, i, nz - 1 - i)

    def chunk(c, carry):
        @pl.when(c < nc)
        def _():
            l_y(c).wait_recv()
            l_f(c).start()

            @pl.when(mid)
            def _():
                m_z(c).wait_recv()
                m_y(c).start()
                m_p(c).start()

        @pl.when(c > 0)
        def _():
            e = c - 1
            l_p(e).wait_recv()
            l_f(e).wait_recv()

            def regress(i, carry):
                zz = jnp.where(mid, near(i), near(nz - 1 - i))
                product(e, zz, zz, a, LF, keep)
                return carry

            lax.fori_loop(0, jnp.where(mid, nz // 2, nz), regress, 0)

        return carry

    lax.fori_loop(0, nc + 1, chunk, 0)

    @pl.when(mid)
    def _():
        def chunk_across(c, carry):
            @pl.when(c < nc)
            def _():
                m_y(c).wait_recv()
                m_f(c).start()

            @pl.when(c > 0)
            def _():
                e = c - 1
                m_p(e).wait_recv()
                m_f(e).wait_recv()

                def regress(i, carry):
                    zz = near(i)
                    product(e, nz - 1 - zz, zz, across, LM, keep_across)
                    return carry

                lax.fori_loop(0, nz // 2, regress, 0)

            return carry

        lax.fori_loop(0, nc + 1, chunk_across, 0)

    def rest(i, c):
        @pl.when(is_late(m * nh + i))
        def _():
            relate(i)

        return c

    lax.fori_loop(0, nh, rest, 0)
    nother.wait_send()
    for i in range(nh):
        p_copy(i).wait_recv()
        kin_out[:, i * cols : (i + 1) * cols] = (KO[i] + PR[i].astype(F32)).astype(BF16)

    def l_sends(c, carry):
        l_y(c).wait_send()
        l_p(c).wait_send()
        l_f(c).wait_send()

        @pl.when(mid)
        def _():
            m_z(c).wait_send()
            m_y(c).wait_send()
            m_p(c).wait_send()
            m_f(c).wait_send()

        @pl.when(keep | keep_across)
        def _():
            r_local(c, 0, a).wait()

        def r_sends(i, carry):
            own = (i == z) & keep
            other = (i == nz - 1 - z) & keep_across

            @pl.when(jnp.logical_not(own | other))
            def _():
                r_copy(c, i, i, a).wait_send()

            return carry

        lax.fori_loop(0, nz, r_sends, 0)

        def r_recvs(i, carry):
            b = m * nh + i
            own = (b == a) & keep
            other = (b == across) & keep_across

            @pl.when(jnp.logical_not(own | other))
            def _():
                remote(
                    R.at[c, 0], reg_out.at[:, window(i, c)], r_send.at[c, 0], r_recv.at[c, i], mk=o
                ).wait_recv()

            return carry

        lax.fori_loop(0, nh, r_recvs, 0)
        return carry

    lax.fori_loop(0, nc, l_sends, 0)
    lax.fori_loop(0, nh, lambda i, c: (p_copy(i).wait_send(), c)[1], 0)

    def g_sends(b, c):
        zz = b // 2
        same = lax.rem(b, 2) == x

        for p in range(2):
            lone = is_end(zz) if p == 0 else False

            @pl.when(same & ((zz == z) | jnp.logical_not(lone)))
            def _():
                go_x(b, p).wait_send()

            @pl.when((same | (lone & (zz == 0))) & (zz <= z) & (z < nz - 1))
            def _():
                go_up(b, p).wait_send()

            @pl.when((same | (lone & (zz == nz - 1))) & (zz >= z) & (z > 0))
            def _():
                go_dn(b, p).wait_send()

        @pl.when(b // nh == o)
        def _():
            go_partner(b).wait_send()

        return c

    lax.fori_loop(0, n, g_sends, 0)

    @pl.when(m == x)
    def _():
        def x_sends(i, c):
            @pl.when(wants(z, i))
            def _():
                nb_x(NF, i).wait_send()

            return c

        lax.fori_loop(0, nz, x_sends, 0)


def store_kernel(kin_ref, reg_ref, kin_out, reg_out, sem):
    copies = [
        pltpu.make_async_copy(src, dst, sem.at[i])
        for i, (src, dst) in enumerate(((kin_ref, kin_out), (reg_ref, reg_out)))
    ]
    for copy in copies:
        copy.start()
    for copy in copies:
        copy.wait()


def kernel_body(n, markers, noncore_geno, noncore_codes, core_geno, core_codes, breed_freqs, core_inverse):
    half = core_geno.shape[1]
    q = half // 2
    cols = core_inverse.shape[1]
    rows = noncore_geno.shape[0]
    nh = nz = n // 2
    nc = 4 if cols % 512 == 0 else 1
    cw = cols // nc
    vmem = pl.BlockSpec(memory_space=pltpu.VMEM)
    anyspace = pl.BlockSpec(memory_space=pl.ANY)
    hbm = pl.BlockSpec(memory_space=pltpu.HBM)
    D = pltpu.SemaphoreType.DMA
    out = jax.ShapeDtypeStruct((rows, nh * cols), BF16)
    held = pltpu.VMEM((rows, nh * cols), BF16)
    related, scores = pl.pallas_call(
        functools.partial(kernel, n, nc, 1.0 / markers),
        out_shape=(held, held),
        in_specs=[hbm] * 6,
        out_specs=(vmem, vmem),
        scratch_shapes=[
            pltpu.VMEM((cols, q), jnp.int32),
            pltpu.VMEM(core_codes.shape, jnp.int32),
            pltpu.VMEM(breed_freqs.shape, F32),
            pltpu.VMEM(noncore_geno.shape, jnp.int32),
            pltpu.VMEM(noncore_codes.shape, jnp.int32),
            pltpu.VMEM((128, q), F32),
            pltpu.VMEM((128, rows), F32),
            pltpu.VMEM((n, 2, q, cols // 2), BF16),
            pltpu.VMEM((nh, 2, q, cols // 2), BF16),
            pltpu.VMEM((n, cols, cols), BF16),
            pltpu.VMEM((q, cols), F32),
            pltpu.VMEM((2, rows, half), BF16),
            pltpu.VMEM((2, rows, half), BF16),
            pltpu.VMEM((nz, 2, rows, half), BF16),
            pltpu.VMEM((nc, 2, half, cw), BF16),
            pltpu.VMEM((nc, 2, half, cw), BF16),
            pltpu.VMEM((nh, rows, cols), BF16),
            pltpu.VMEM((nh, rows, cols), BF16),
            pltpu.VMEM((nh, rows, cols), F32),
            pltpu.VMEM((nc, nz, rows, cw), BF16),
            D((2,)), D((4,)), D((n,)), D((n, 2)), D((n, 2)), D((n, 2)), D((n, 2)), D((nh,)), D((nh,)),
            D((2,)), D((2,)), D, D((nz,)), D((nz,)), D((nz,)), D((3, nc)), D((3, nc)),
            D((4, nc)), D((4, nc)),
            D((nh,)), D((nh,)), D((nc, nz)), D((nc, nh)), D((nc,)),
        ],
        compiler_params=pltpu.CompilerParams(
            collective_id=0, has_side_effects=True, vmem_limit_bytes=54 * 1024 * 1024
        ),
    )(core_geno, core_codes, breed_freqs, noncore_geno, noncore_codes, core_inverse)
    return pl.pallas_call(
        store_kernel,
        out_shape=(out, out),
        in_specs=[vmem] * 2,
        out_specs=(anyspace, anyspace),
        scratch_shapes=[D((2,))],
    )(*(pltpu.with_memory_space_constraint(v, pltpu.VMEM) for v in (related, scores)))


def solution(mesh):
    in_specs = (
        P(("grp", "anim"), "mark"),
        P(None, ("grp", "anim")),
        P("anim", "mark"),
        P(None, "anim"),
        P(None, "mark"),
        P(None, "anim"),
    )
    out_specs = (P(("grp", "anim"), "mark"), P(("grp", "anim"), "mark"))
    n = mesh.shape["anim"]

    def body(*args):
        half, cols, rows = args[2].shape[1], args[5].shape[1], args[0].shape[0]
        markers = half * mesh.shape["mark"]
        fits = (
            mesh.shape["grp"] == 2 and mesh.shape["mark"] == 2 and n == 8
            and half % 256 == 0 and cols % 256 == 0 and rows % 128 == 0 and args[4].shape[0] <= 128
            and args[2].shape[0] == cols and n * cols * cols * 2 <= 24 * 2**20
        )
        if fits:
            return kernel_body(n, markers, *args)
        return plain_body(markers, *args)

    return jax.shard_map(body, mesh=mesh, in_specs=in_specs, out_specs=out_specs, check_vma=False)
```

```python
import functools

import jax
import jax.numpy as jnp
from jax import lax
from jax.experimental import pallas as pl
from jax.experimental.pallas import tpu as pltpu
from jax.sharding import PartitionSpec as P

MESH = pl.DeviceIdType.MESH
F32 = jnp.float32
BF16 = jnp.bfloat16


def centre_value(genotypes, breed_codes, breed_freqs):
    fractions = breed_codes.astype(F32) / 32.0
    expected = lax.dot_general(
        fractions, breed_freqs, (((0,), (0,)), ((), ())), precision=lax.Precision.HIGHEST
    )
    return (genotypes.astype(F32) - 2.0 * expected).astype(BF16)


def plain_body(markers, noncore_geno, noncore_codes, core_geno, core_codes, breed_freqs, core_inverse):
    noncore_z = centre_value(noncore_geno, noncore_codes, breed_freqs)
    core_z = centre_value(core_geno, core_codes, breed_freqs)
    rows = lax.all_gather(core_z, "anim", axis=0, tiled=True)
    related = (
        lax.dot_general(noncore_z, rows, (((1,), (1,)), ((), ())), preferred_element_type=F32) / markers
    )
    loading = lax.dot_general(rows, core_inverse, (((0,), (0,)), ((), ())), preferred_element_type=F32)
    scores = (
        jnp.dot(
            noncore_z,
            lax.all_gather(loading.astype(BF16), "anim", axis=1, tiled=True),
            preferred_element_type=F32,
        )
        / markers
    )
    return tuple(
        lax.psum_scatter(v.astype(BF16), "mark", scatter_dimension=1, tiled=True) for v in (related, scores)
    )


def kernel(
    n, nc, scale, geno_hbm, codes_hbm, freqs_hbm, ngeno_hbm, ncodes_hbm, inv_hbm, kin_out, reg_out,
    RAW, codes, freqs, ngeno, ncodes, TF, TC, G, H, GO, HO, INV, ACC, NF, NO, NB, LF, LM, PO, PR, KO, R,
    raw_sem, in_sem, inv_sem, g_recv, up_send, dn_send, x_send, h_send, h_recv, ho_send, ho_recv,
    n_send, n_recv, nb_loc, nb_zsend, nb_xsend, nb_recv, l_send, l_recv, m_send, m_recv,
    p_send, p_recv, r_send, r_recv, r_loc,
):
    nz, nh = n // 2, n // 2
    y, a, m = lax.axis_index("grp"), lax.axis_index("anim"), lax.axis_index("mark")
    z, x = a // 2, lax.rem(a, 2)
    o = 1 - m
    q, hc = G.shape[2:]
    cols = 2 * hc
    breeds = freqs.shape[0]
    cw = cols // nc
    here = pl.ds(pl.multiple_of(y * q, q), q)
    there = pl.ds(pl.multiple_of((1 - y) * q, q), q)
    low = z < nz // 2
    mid = (z > 0) & (z < nz - 1)
    end = jnp.logical_not(mid)
    across = 2 * (nz - 1 - z) + x
    beside = a + 1 - 2 * x
    block = jnp.where(end & (m != x), beside, a)

    def is_end(zz):
        return (zz == 0) | (zz == nz - 1)

    def remote(src, dst, ss, rs, g=None, an=None, mk=None):
        return pltpu.make_async_remote_copy(
            src_ref=src, dst_ref=dst, send_sem=ss, recv_sem=rs,
            device_id=(y if g is None else g, a if an is None else an, m if mk is None else mk),
            device_id_type=MESH,
        )

    barrier = pltpu.get_barrier_semaphore()

    def greet(g=None, an=None, mk=None):
        pl.semaphore_signal(
            barrier, inc=1,
            device_id=(y if g is None else g, a if an is None else an, m if mk is None else mk),
            device_id_type=MESH,
        )

    greet(mk=o)
    greet(an=a + 1 - 2 * x)
    greet(g=1 - y)

    @pl.when(z < nz - 1)
    def _():
        greet(an=a + 2)

    @pl.when(z > 0)
    def _():
        greet(an=a - 2)

    def inv_copy(b):
        return pltpu.make_async_copy(inv_hbm.at[pl.ds(b * cols, cols)], INV.at[b], inv_sem.at[b])

    raw = [
        pltpu.make_async_copy(geno_hbm.at[pl.ds(p * hc, hc)], RAW.at[pl.ds(p * hc, hc)], raw_sem.at[p])
        for p in range(2)
    ]
    small = [
        pltpu.make_async_copy(src, dst, in_sem.at[i])
        for i, (src, dst) in enumerate(
            ((codes_hbm, codes), (freqs_hbm, freqs), (ngeno_hbm, ngeno), (ncodes_hbm, ncodes))
        )
    ]
    for copy in raw + small:
        copy.start()

    lax.fori_loop(0, n, lambda i, c: (inv_copy(lax.rem(a + i, n)).start(), c)[1], 0)

    def go_up(b, p):
        return remote(G.at[b, p], G.at[b, p], up_send.at[b, p], g_recv.at[b, p], an=a + 2)

    def go_dn(b, p):
        return remote(G.at[b, p], G.at[b, p], dn_send.at[b, p], g_recv.at[b, p], an=a - 2)

    def go_x(b, p):
        return remote(G.at[b, p], G.at[b, p], x_send.at[b, p], g_recv.at[b, p], an=a + 1 - 2 * x)

    def go_partner(b):
        i = lax.rem(b, nh)
        return remote(G.at[b], H.at[i], h_send.at[i], h_recv.at[i], mk=o)

    TF[...] = jnp.zeros_like(TF)
    TC[...] = jnp.zeros_like(TC)
    small[0].wait()
    small[1].wait()
    TF[:breeds, :] = freqs[...]

    def centre(p, markers, freq_t, dst):
        for t in range(0, hc, 128):
            at = slice(p * hc + t, p * hc + t + 128)
            expected = freq_t[:, 0:1] * (codes[0:1, at].astype(F32) / 32.0)
            for b in range(1, breeds):
                expected += freq_t[:, b : b + 1] * (codes[b : b + 1, at].astype(F32) / 32.0)
            dst[:, t : t + 128] = (RAW[at, markers].astype(F32).T - 2.0 * expected).astype(BF16)

    freq_t = TF[:, here].T
    for p in range(2):
        raw[p].wait()
        centre(p, here, freq_t, G.at[a, p])
        if p == 0:
            pl.semaphore_wait(barrier, 5 - jnp.where(mid, 0, 1))

        @pl.when(z < nz - 1)
        def _():
            go_up(a, p).start()

        @pl.when(z > 0)
        def _():
            go_dn(a, p).start()

        go_x(a, p).start()

    small[2].wait()
    small[3].wait()
    TC[:breeds, :] = ncodes[...].astype(F32) / 32.0
    code_t = TC[...].T
    expected = code_t[:, 0:1] * freqs[0:1, :]
    for b in range(1, breeds):
        expected += code_t[:, b : b + 1] * freqs[b : b + 1, :]
    NF[m] = (ngeno[...].astype(F32) - 2.0 * expected).astype(BF16)
    npart = remote(NF.at[m], NF.at[m], n_send.at[0], n_recv.at[0], mk=o)
    npart.start()
    n_y = remote(NF.at[m, :, there], NO.at[m], n_send.at[1], n_recv.at[1], g=1 - y)
    n_y.start()
    freq_t = TF[:, there].T
    for p in range(2):
        centre(p, there, freq_t, GO.at[p])
    own_partner = remote(GO, HO, ho_send, ho_recv, mk=o)

    @pl.when(a // nh == o)
    def _():
        own_partner.start()

    ACC[...] = jnp.zeros_like(ACC)
    npart.wait_send()
    remote(NF.at[o], NF.at[o], n_send.at[0], n_recv.at[0], mk=o).wait_recv()
    n_y.wait_recv()
    n_f = remote(NO.at[m], NO.at[m], n_send.at[2], n_recv.at[2], mk=o)
    n_f.start()

    def near(i):
        return jnp.where(low, i, nz - 1 - i)

    def nb_in(src, i):
        return remote(
            src, NB.at[i], nb_zsend.at[0, i], nb_recv.at[i], an=jnp.where(mid, across, 2 * near(1) + x)
        )

    def nb_out(src, i):
        return remote(src, NB.at[i], nb_zsend.at[1, i], nb_recv.at[i], an=2 * near(0) + x)

    def nb_x(src, i):
        return remote(src, NB.at[i], nb_xsend.at[i], nb_recv.at[i], an=a + 1 - 2 * x)

    nb_local = pltpu.make_async_copy(NF, NB.at[z], nb_loc)

    def nb_c(i):
        return remote(NB.at[i], NB.at[i], nb_xsend.at[i], nb_recv.at[i], mk=o)

    @pl.when(end | (m == x))
    def _():
        nb_local.start()

    def p_copy(i):
        return remote(PO.at[i], PR.at[i], p_send.at[i], p_recv.at[i], g=1 - y)

    def product(ref, p, mine, his):
        return jnp.dot(ref[m], mine, preferred_element_type=F32) + jnp.dot(
            ref[o], his, preferred_element_type=F32
        )

    def relate(i):
        b = m * nh + i
        go_partner(b).wait_recv()
        for p in range(2):
            span = slice(p * hc, (p + 1) * hc)
            PO[i, :, span] = (product(NO, p, G[b, p], H[i, p]) * scale).astype(BF16)
            KO[i, :, span] = product(NF.at[:, :, here], p, G[b, p], H[i, p]) * scale
        p_copy(i).start()

    def relate_own():
        i = lax.rem(a, nh)
        go_partner(a).wait_recv()
        own_partner.wait_recv()
        for p in range(2):
            span = slice(p * hc, (p + 1) * hc)
            KO[i, :, span] = (
                product(NF.at[:, :, here], p, G[a, p], H[i, p])
                + product(NF.at[:, :, there], p, GO[p], HO[p])
            ) * scale

    late = nz - 1

    def is_late(b):
        side = jnp.where(lax.rem(b, 2) == x, 0, 1)
        d = jnp.abs(b // 2 - z) + side
        return d >= late

    def step(s, c):
        def lift(j, c):
            zz = z + (s - 1) * (2 * j - 1)

            @pl.when((s > 0) & (zz == j * (nz - 1)))
            def _():
                b = 2 * zz + 1 - x
                go_x(b, 1).wait_recv()

                @pl.when((j == 0) & (z < nz - 1))
                def _():
                    go_up(b, 1).start()

                @pl.when((j == 1) & (z > 0))
                def _():
                    go_dn(b, 1).start()

            return c

        def hop(k, c):
            j, p = lax.rem(k, 2), k // 2
            zz = z + s * (2 * j - 1)

            @pl.when((s > 0) & (zz >= 0) & (zz < nz))
            def _():
                b = 2 * zz + x
                go_up(b, p).wait_recv()

                @pl.when((j == 0) & (z < nz - 1))
                def _():
                    go_up(b, p).start()

                @pl.when((j == 1) & (z > 0))
                def _():
                    go_dn(b, p).start()

                @pl.when((p == 0) | jnp.logical_not(is_end(zz)))
                def _():
                    go_x(b, p).start()

            return c

        lax.fori_loop(0, 2, hop, 0)
        lax.fori_loop(0, 2, lift, 0)
        lax.fori_loop(2, 4, hop, 0)

        @pl.when((s == 1) & (m == x))
        def _():
            nb_in(NF, z).start()

            @pl.when(mid)
            def _():
                nb_x(NF, z).start()

        @pl.when((s == late - 1) & (m == x) & mid)
        def _():
            i = near(0)
            nb_in(NB.at[i], i).wait_recv()
            nb_in(NB.at[i], i).start()
            nb_x(NB.at[i], i).start()

        @pl.when((s == late) & (m == x) & mid)
        def _():
            nb_out(NF, z).start()
            for i in (nz - 1 - z, near(nz - 1)):
                nb_in(NB.at[i], i).wait_recv()
                nb_out(NB.at[i], i).start()

        def use(k, c):
            j, side = lax.rem(k, 2), k // 2
            d = s - side
            zz = z + d * (2 * j - 1)

            @pl.when((d >= 0) & (zz >= 0) & (zz < nz) & ((d > 0) | (j == 0)))
            def _():
                b = 2 * zz + x + side * (1 - 2 * x)

                @pl.when(side == 1)
                def _():
                    go_x(b, 0).wait_recv()

                    @pl.when(jnp.logical_not(is_end(zz)))
                    def _():
                        go_x(b, 1).wait_recv()

                @pl.when(b // nh == o)
                def _():
                    go_partner(b).start()

                inv_copy(b).wait()
                first, second = G[b, 0], G[b, 1]
                width = 256 if cols % 256 == 0 else 128
                for t in range(0, cols, width):
                    ACC[:, t : t + width] += jnp.dot(
                        first, INV[b, :hc, t : t + width], preferred_element_type=F32
                    ) + jnp.dot(second, INV[b, hc:, t : t + width], preferred_element_type=F32)

                @pl.when(s == 0)
                def _():
                    n_f.wait_recv()

                    @pl.when(b // nh == m)
                    def _():
                        relate_own()

                @pl.when((b // nh == m) & (s > 0) & jnp.logical_not(is_late(b)))
                def _():
                    relate(lax.rem(b, nh))

            return c

        lax.fori_loop(0, 4, use, 0)

        return c

    lax.fori_loop(0, nz + 1, step, 0)

    def l_y(c):
        return remote(LF.at[c, m, here], LF.at[c, m, here], l_send.at[0, c], l_recv.at[0, c], g=1 - y)

    def l_p(c):
        return remote(LF.at[c, m, here], LF.at[c, m, here], l_send.at[1, c], l_recv.at[1, c], mk=o)

    def l_f(c):
        return remote(LF.at[c, m, there], LF.at[c, m, there], l_send.at[2, c], l_recv.at[2, c], mk=o)

    def m_z(c):
        return remote(LF.at[c, m, here], LM.at[c, m, here], m_send.at[3, c], m_recv.at[3, c], an=across)

    def m_y(c):
        return remote(LM.at[c, m, here], LM.at[c, m, here], m_send.at[0, c], m_recv.at[0, c], g=1 - y)

    def m_p(c):
        return remote(LM.at[c, m, here], LM.at[c, m, here], m_send.at[1, c], m_recv.at[1, c], mk=o)

    def m_f(c):
        return remote(LM.at[c, m, there], LM.at[c, m, there], m_send.at[2, c], m_recv.at[2, c], mk=o)

    def e_h(c):
        return remote(
            LF.at[c, m, here], LM.at[c, m, here], m_send.at[0, c], m_recv.at[2 * m, c], an=beside, mk=x
        )

    def e_t(c):
        return remote(
            LF.at[c, m, there], LM.at[c, m, there], m_send.at[1, c], m_recv.at[2 * m + 1, c], an=beside, mk=x
        )

    for c in range(nc):
        LF[c, m, here, :] = ACC[:, c * cw : (c + 1) * cw].astype(BF16)

        @pl.when(mid)
        def _():
            m_z(c).start()

        l_y(c).start()

        @pl.when(mid | (m != x))
        def _():
            l_p(c).start()

        @pl.when(end)
        def _():
            e_h(c).start()

    def pass_on(zz):
        @pl.when(end & (m == x) & (zz != z))
        def _():
            nb_c(zz).wait_recv()
            nb_c(zz).start()

    def arrive(zz):
        @pl.when((end | (m == x)) & (zz == z))
        def _():
            nb_local.wait()

        @pl.when((m != x) & (mid | (zz != z)))
        def _():
            nb_c(zz).wait_recv()

    def window(b, c):
        return pl.ds(pl.multiple_of(lax.rem(b, nh) * cols + c * cw, cw), cw)

    def r_copy(c, slot, zz, b):
        return remote(
            R.at[c, slot], reg_out.at[:, window(b, c)], r_send.at[c, slot], r_recv.at[c, lax.rem(b, nh)],
            an=2 * zz + jnp.where(mid, m, x), mk=b // nh,
        )

    def r_local(c, slot, b):
        return pltpu.make_async_copy(R.at[c, slot], reg_out.at[:, window(b, c)], r_loc.at[c])

    keep = (end | (m == x)) & (a // nh == m)
    keep_across = mid & (m == x) & (across // nh == m)

    def score(c, slot, zz, b, ref, stays):
        R[c, slot] = (
            (
                jnp.dot(NB[zz, 0], ref[c, 0], preferred_element_type=F32)
                + jnp.dot(NB[zz, 1], ref[c, 1], preferred_element_type=F32)
            )
            * scale
        ).astype(BF16)

        @pl.when((zz == z) & stays)
        def _():
            r_local(c, slot, b).start()

        @pl.when((zz != z) | jnp.logical_not(stays))
        def _():
            r_copy(c, slot, zz, b).start()

    def rest(i, c):
        @pl.when(is_late(m * nh + i))
        def _():
            relate(i)

        return c

    @pl.when(end)
    def _():
        lax.fori_loop(0, nh, rest, 0)

    def chunk(c, carry):
        @pl.when(c < nc)
        def _():
            l_y(c).wait_recv()

            @pl.when(mid | (m != x))
            def _():
                l_f(c).start()

            @pl.when(end)
            def _():
                e_t(c).start()

            @pl.when(mid)
            def _():
                m_z(c).wait_recv()
                m_y(c).start()
                m_p(c).start()

            @pl.when(c == 0)
            def _():
                pass_on(near(1))

        @pl.when(c > 0)
        def _():
            e = c - 1

            def regress(ref, i, carry):
                zz = near(i)

                @pl.when(e == 0)
                def _():
                    @pl.when(i != 1)
                    def _():
                        pass_on(zz)

                    arrive(zz)

                score(e, zz, zz, block, ref, keep)
                return carry

            @pl.when(mid | (m == x))
            def _():
                l_p(e).wait_recv()
                l_f(e).wait_recv()
                lax.fori_loop(0, jnp.where(mid, nz // 2, nz), functools.partial(regress, LF), 0)

            @pl.when(end & (m != x))
            def _():
                def part(k, carry):
                    at = pl.ds(pl.multiple_of((y + lax.rem(k, 2) * (1 - 2 * y)) * q, q), q)
                    remote(
                        LM.at[e, k // 2, at], LM.at[e, k // 2, at], m_send.at[0, e], m_recv.at[k, e], mk=o
                    ).wait_recv()
                    return carry

                lax.fori_loop(0, 4, part, 0)
                lax.fori_loop(0, nz, functools.partial(regress, LM), 0)

        return carry

    lax.fori_loop(0, nc + 1, chunk, 0)

    @pl.when(mid)
    def _():
        lax.fori_loop(0, nh, rest, 0)

        def chunk_across(c, carry):
            @pl.when(c < nc)
            def _():
                m_y(c).wait_recv()
                m_f(c).start()

            @pl.when(c > 0)
            def _():
                e = c - 1
                m_p(e).wait_recv()
                m_f(e).wait_recv()

                def regress(i, carry):
                    zz = near(i)
                    score(e, nz - 1 - zz, zz, across, LM, keep_across)
                    return carry

                lax.fori_loop(0, nz // 2, regress, 0)

            return carry

        lax.fori_loop(0, nc + 1, chunk_across, 0)

    n_y.wait_send()
    n_f.wait_send()

    @pl.when(a // nh == o)
    def _():
        own_partner.wait_send()

    for i in range(nh):
        span = slice(i * cols, (i + 1) * cols)

        @pl.when(m * nh + i == a)
        def _():
            kin_out[:, span] = KO[i].astype(BF16)

        @pl.when(m * nh + i != a)
        def _():
            p_copy(i).wait_recv()
            kin_out[:, span] = (KO[i] + PR[i].astype(F32)).astype(BF16)

    def l_sends(c, carry):
        l_y(c).wait_send()

        @pl.when(mid | (m != x))
        def _():
            l_p(c).wait_send()
            l_f(c).wait_send()

        @pl.when(end)
        def _():
            e_h(c).wait_send()
            e_t(c).wait_send()

        @pl.when(mid)
        def _():
            m_z(c).wait_send()
            m_y(c).wait_send()
            m_p(c).wait_send()
            m_f(c).wait_send()

        @pl.when(keep | keep_across)
        def _():
            r_local(c, 0, a).wait()

        def r_sends(i, carry):
            own = (i == z) & keep
            other = (i == nz - 1 - z) & keep_across

            @pl.when(jnp.logical_not(own | other))
            def _():
                r_copy(c, i, i, a).wait_send()

            return carry

        lax.fori_loop(0, nz, r_sends, 0)

        def r_recvs(i, carry):
            b = m * nh + i
            own = (b == block) & keep
            other = (b == across) & keep_across

            @pl.when(jnp.logical_not(own | other))
            def _():
                remote(
                    R.at[c, 0], reg_out.at[:, window(i, c)], r_send.at[c, 0], r_recv.at[c, i], mk=o
                ).wait_recv()

            return carry

        lax.fori_loop(0, nh, r_recvs, 0)
        return carry

    lax.fori_loop(0, nc, l_sends, 0)

    def p_sends(i, c):
        @pl.when(m * nh + i != a)
        def _():
            p_copy(i).wait_send()

        return c

    lax.fori_loop(0, nh, p_sends, 0)

    def g_sends(b, c):
        zz = b // 2
        same = lax.rem(b, 2) == x

        for p in range(2):
            lone = is_end(zz) if p == 1 else False

            @pl.when(same & ((zz == z) | jnp.logical_not(lone)))
            def _():
                go_x(b, p).wait_send()

            @pl.when((same | (lone & (zz == 0))) & (zz <= z) & (z < nz - 1))
            def _():
                go_up(b, p).wait_send()

            @pl.when((same | (lone & (zz == nz - 1))) & (zz >= z) & (z > 0))
            def _():
                go_dn(b, p).wait_send()

        @pl.when(b // nh == o)
        def _():
            go_partner(b).wait_send()

        return c

    lax.fori_loop(0, n, g_sends, 0)

    @pl.when(m == x)
    def _():
        nb_in(NF, z).wait_send()

        @pl.when(mid)
        def _():
            nb_in(NF, near(0)).wait_send()
            nb_x(NF, z).wait_send()
            nb_x(NF, near(0)).wait_send()
            for i in (z, nz - 1 - z, near(nz - 1)):
                nb_out(NF, i).wait_send()

        @pl.when(end)
        def _():
            for i in range(1, nz):
                nb_c(near(i)).wait_send()


def store_kernel(kin_ref, reg_ref, kin_out, reg_out, sem):
    rows = kin_ref.shape[0] // 4
    copies = [
        pltpu.make_async_copy(src.at[pl.ds(k * rows, rows)], dst.at[pl.ds(k * rows, rows)], sem.at[i, k])
        for i, (src, dst) in enumerate(((kin_ref, kin_out), (reg_ref, reg_out)))
        for k in range(4)
    ]
    for copy in copies:
        copy.start()
    for copy in copies:
        copy.wait()


def kernel_body(n, markers, noncore_geno, noncore_codes, core_geno, core_codes, breed_freqs, core_inverse):
    half = core_geno.shape[1]
    q = half // 2
    cols = core_inverse.shape[1]
    rows = noncore_geno.shape[0]
    nh = nz = n // 2
    nc = 4 if cols % 512 == 0 else 1
    cw = cols // nc
    vmem = pl.BlockSpec(memory_space=pltpu.VMEM)
    anyspace = pl.BlockSpec(memory_space=pl.ANY)
    hbm = pl.BlockSpec(memory_space=pltpu.HBM)
    D = pltpu.SemaphoreType.DMA
    out = jax.ShapeDtypeStruct((rows, nh * cols), BF16)
    held = pltpu.VMEM((rows, nh * cols), BF16)
    related, scores = pl.pallas_call(
        functools.partial(kernel, n, nc, 1.0 / markers),
        out_shape=(held, held),
        in_specs=[hbm] * 6,
        out_specs=(vmem, vmem),
        scratch_shapes=[
            pltpu.VMEM((cols, half), jnp.int32),
            pltpu.VMEM(core_codes.shape, jnp.int32),
            pltpu.VMEM(breed_freqs.shape, F32),
            pltpu.VMEM(noncore_geno.shape, jnp.int32),
            pltpu.VMEM(noncore_codes.shape, jnp.int32),
            pltpu.VMEM((128, half), F32),
            pltpu.VMEM((128, rows), F32),
            pltpu.VMEM((n, 2, q, cols // 2), BF16),
            pltpu.VMEM((nh, 2, q, cols // 2), BF16),
            pltpu.VMEM((2, q, cols // 2), BF16),
            pltpu.VMEM((2, q, cols // 2), BF16),
            pltpu.VMEM((n, cols, cols), BF16),
            pltpu.VMEM((q, cols), F32),
            pltpu.VMEM((2, rows, half), BF16),
            pltpu.VMEM((2, rows, q), BF16),
            pltpu.VMEM((nz, 2, rows, half), BF16),
            pltpu.VMEM((nc, 2, half, cw), BF16),
            pltpu.VMEM((nc, 2, half, cw), BF16),
            pltpu.VMEM((nh, rows, cols), BF16),
            pltpu.VMEM((nh, rows, cols), BF16),
            pltpu.VMEM((nh, rows, cols), F32),
            pltpu.VMEM((nc, nz, rows, cw), BF16),
            D((2,)), D((4,)), D((n,)), D((n, 2)), D((n, 2)), D((n, 2)), D((n, 2)), D((nh,)), D((nh,)), D, D,
            D((3,)), D((3,)), D, D((2, nz)), D((nz,)), D((nz,)), D((3, nc)), D((3, nc)),
            D((4, nc)), D((4, nc)),
            D((nh,)), D((nh,)), D((nc, nz)), D((nc, nh)), D((nc,)),
        ],
        compiler_params=pltpu.CompilerParams(
            collective_id=0, has_side_effects=True, vmem_limit_bytes=54 * 1024 * 1024
        ),
    )(core_geno, core_codes, breed_freqs, noncore_geno, noncore_codes, core_inverse)
    return pl.pallas_call(
        store_kernel,
        out_shape=(out, out),
        in_specs=[vmem] * 2,
        out_specs=(anyspace, anyspace),
        scratch_shapes=[D((2, 4))],
    )(*(pltpu.with_memory_space_constraint(v, pltpu.VMEM) for v in (related, scores)))


def solution(mesh):
    in_specs = (
        P(("grp", "anim"), "mark"),
        P(None, ("grp", "anim")),
        P("anim", "mark"),
        P(None, "anim"),
        P(None, "mark"),
        P(None, "anim"),
    )
    out_specs = (P(("grp", "anim"), "mark"), P(("grp", "anim"), "mark"))
    n = mesh.shape["anim"]

    def body(*args):
        half, cols, rows = args[2].shape[1], args[5].shape[1], args[0].shape[0]
        markers = half * mesh.shape["mark"]
        fits = (
            mesh.shape["grp"] == 2 and mesh.shape["mark"] == 2 and n == 8
            and half % 256 == 0 and cols % 256 == 0 and rows % 128 == 0 and args[4].shape[0] <= 128
            and args[2].shape[0] == cols and n * cols * cols * 2 <= 24 * 2**20
        )
        if fits:
            return kernel_body(n, markers, *args)
        return plain_body(markers, *args)

    return jax.shard_map(body, mesh=mesh, in_specs=in_specs, out_specs=out_specs, check_vma=False)
```

```python
import functools

import jax
import jax.numpy as jnp
from jax import lax
from jax.experimental import pallas as pl
from jax.experimental.pallas import tpu as pltpu
from jax.sharding import PartitionSpec as P

MESH = pl.DeviceIdType.MESH
F32 = jnp.float32
BF16 = jnp.bfloat16


def centre_value(genotypes, breed_codes, breed_freqs):
    fractions = breed_codes.astype(F32) / 32.0
    expected = lax.dot_general(
        fractions, breed_freqs, (((0,), (0,)), ((), ())), precision=lax.Precision.HIGHEST
    )
    return (genotypes.astype(F32) - 2.0 * expected).astype(BF16)


def plain_body(markers, noncore_geno, noncore_codes, core_geno, core_codes, breed_freqs, core_inverse):
    noncore_z = centre_value(noncore_geno, noncore_codes, breed_freqs)
    core_z = centre_value(core_geno, core_codes, breed_freqs)
    rows = lax.all_gather(core_z, "anim", axis=0, tiled=True)
    related = (
        lax.dot_general(noncore_z, rows, (((1,), (1,)), ((), ())), preferred_element_type=F32) / markers
    )
    loading = lax.dot_general(rows, core_inverse, (((0,), (0,)), ((), ())), preferred_element_type=F32)
    scores = (
        jnp.dot(
            noncore_z,
            lax.all_gather(loading.astype(BF16), "anim", axis=1, tiled=True),
            preferred_element_type=F32,
        )
        / markers
    )
    return tuple(
        lax.psum_scatter(v.astype(BF16), "mark", scatter_dimension=1, tiled=True) for v in (related, scores)
    )


def kernel(
    n, nc, scale, geno_hbm, codes_hbm, freqs_hbm, ngeno_hbm, ncodes_hbm, inv_hbm, kin_out, reg_out,
    RAW, codes, freqs, ngeno, ncodes, TF, TC, G, H, GO, HO, INV, ACC, NF, NO, NB, LF, LM, PO, PR, KO, R,
    raw_sem, in_sem, inv_sem, g_recv, up_send, dn_send, x_send, h_send, h_recv, ho_send, ho_recv,
    n_send, n_recv, nb_loc, nb_zsend, nb_xsend, nb_recv, l_send, l_recv, m_send, m_recv,
    p_send, p_recv, r_send, r_recv, r_loc,
):
    nz, nh = n // 2, n // 2
    y, a, m = lax.axis_index("grp"), lax.axis_index("anim"), lax.axis_index("mark")
    z, x = a // 2, lax.rem(a, 2)
    o = 1 - m
    q, hc = G.shape[2:]
    cols = 2 * hc
    breeds = freqs.shape[0]
    cw = cols // nc
    here = pl.ds(pl.multiple_of(y * q, q), q)
    there = pl.ds(pl.multiple_of((1 - y) * q, q), q)
    low = z < nz // 2
    mid = (z > 0) & (z < nz - 1)
    end = jnp.logical_not(mid)
    across = 2 * (nz - 1 - z) + x
    beside = a + 1 - 2 * x
    block = jnp.where(end & (m != x), beside, a)

    def is_end(zz):
        return (zz == 0) | (zz == nz - 1)

    def remote(src, dst, ss, rs, g=None, an=None, mk=None):
        return pltpu.make_async_remote_copy(
            src_ref=src, dst_ref=dst, send_sem=ss, recv_sem=rs,
            device_id=(y if g is None else g, a if an is None else an, m if mk is None else mk),
            device_id_type=MESH,
        )

    barrier = pltpu.get_barrier_semaphore()

    def greet(g=None, an=None, mk=None):
        pl.semaphore_signal(
            barrier, inc=1,
            device_id=(y if g is None else g, a if an is None else an, m if mk is None else mk),
            device_id_type=MESH,
        )

    greet(mk=o)
    greet(an=a + 1 - 2 * x)
    greet(g=1 - y)

    @pl.when(z < nz - 1)
    def _():
        greet(an=a + 2)

    @pl.when(z > 0)
    def _():
        greet(an=a - 2)

    def inv_copy(b):
        return pltpu.make_async_copy(inv_hbm.at[pl.ds(b * cols, cols)], INV.at[b], inv_sem.at[b])

    raw = [
        pltpu.make_async_copy(geno_hbm.at[pl.ds(p * hc, hc)], RAW.at[pl.ds(p * hc, hc)], raw_sem.at[p])
        for p in range(2)
    ]
    small = [
        pltpu.make_async_copy(src, dst, in_sem.at[i])
        for i, (src, dst) in enumerate(
            ((codes_hbm, codes), (freqs_hbm, freqs), (ngeno_hbm, ngeno), (ncodes_hbm, ncodes))
        )
    ]
    for copy in raw + small:
        copy.start()

    lax.fori_loop(0, n, lambda i, c: (inv_copy(lax.rem(a + i, n)).start(), c)[1], 0)

    def go_up(b, p):
        return remote(G.at[b, p], G.at[b, p], up_send.at[b, p], g_recv.at[b, p], an=a + 2)

    def go_dn(b, p):
        return remote(G.at[b, p], G.at[b, p], dn_send.at[b, p], g_recv.at[b, p], an=a - 2)

    def go_x(b, p):
        return remote(G.at[b, p], G.at[b, p], x_send.at[b, p], g_recv.at[b, p], an=a + 1 - 2 * x)

    def go_partner(b):
        i = lax.rem(b, nh)
        return remote(G.at[b], H.at[i], h_send.at[i], h_recv.at[i], mk=o)

    TF[...] = jnp.zeros_like(TF)
    TC[...] = jnp.zeros_like(TC)
    small[0].wait()
    small[1].wait()
    TF[:breeds, :] = freqs[...]

    def centre(p, markers, freq_t, dst):
        for t in range(0, hc, 128):
            at = slice(p * hc + t, p * hc + t + 128)
            expected = freq_t[:, 0:1] * (codes[0:1, at].astype(F32) / 32.0)
            for b in range(1, breeds):
                expected += freq_t[:, b : b + 1] * (codes[b : b + 1, at].astype(F32) / 32.0)
            dst[:, t : t + 128] = (RAW[at, markers].astype(F32).T - 2.0 * expected).astype(BF16)

    freq_t = TF[:, here].T
    for p in range(2):
        raw[p].wait()
        centre(p, here, freq_t, G.at[a, p])
        if p == 0:
            pl.semaphore_wait(barrier, 5 - jnp.where(mid, 0, 1))

        @pl.when(z < nz - 1)
        def _():
            go_up(a, p).start()

        @pl.when(z > 0)
        def _():
            go_dn(a, p).start()

        go_x(a, p).start()

    small[2].wait()
    small[3].wait()
    TC[:breeds, :] = ncodes[...].astype(F32) / 32.0
    code_t = TC[...].T
    expected = code_t[:, 0:1] * freqs[0:1, :]
    for b in range(1, breeds):
        expected += code_t[:, b : b + 1] * freqs[b : b + 1, :]
    NF[m] = (ngeno[...].astype(F32) - 2.0 * expected).astype(BF16)
    npart = remote(NF.at[m], NF.at[m], n_send.at[0], n_recv.at[0], mk=o)
    npart.start()
    n_y = remote(NF.at[m, :, there], NO.at[m], n_send.at[1], n_recv.at[1], g=1 - y)
    n_y.start()
    freq_t = TF[:, there].T
    for p in range(2):
        centre(p, there, freq_t, GO.at[p])
    own_partner = remote(GO, HO, ho_send, ho_recv, mk=o)

    @pl.when(a // nh == o)
    def _():
        own_partner.start()

    ACC[...] = jnp.zeros_like(ACC)
    npart.wait_send()
    remote(NF.at[o], NF.at[o], n_send.at[0], n_recv.at[0], mk=o).wait_recv()
    n_y.wait_recv()
    n_f = remote(NO.at[m], NO.at[m], n_send.at[2], n_recv.at[2], mk=o)
    n_f.start()

    def near(i):
        return jnp.where(low, i, nz - 1 - i)

    def nb_in(src, i):
        return remote(
            src, NB.at[i], nb_zsend.at[0, i], nb_recv.at[i], an=jnp.where(mid, across, 2 * near(1) + x)
        )

    def nb_out(src, i):
        return remote(src, NB.at[i], nb_zsend.at[1, i], nb_recv.at[i], an=2 * near(0) + x)

    def nb_x(src, i):
        return remote(src, NB.at[i], nb_xsend.at[i], nb_recv.at[i], an=a + 1 - 2 * x)

    nb_local = pltpu.make_async_copy(NF, NB.at[z], nb_loc)

    def nb_c(i):
        return remote(NB.at[i], NB.at[i], nb_xsend.at[i], nb_recv.at[i], mk=o)

    @pl.when(end | (m == x))
    def _():
        nb_local.start()

    def p_copy(i):
        return remote(PO.at[i], PR.at[i], p_send.at[i], p_recv.at[i], g=1 - y)

    def product(ref, p, mine, his):
        return jnp.dot(ref[m], mine, preferred_element_type=F32) + jnp.dot(
            ref[o], his, preferred_element_type=F32
        )

    def relate(i):
        b = m * nh + i
        go_partner(b).wait_recv()
        for p in range(2):
            span = slice(p * hc, (p + 1) * hc)
            PO[i, :, span] = (product(NO, p, G[b, p], H[i, p]) * scale).astype(BF16)
            KO[i, :, span] = product(NF.at[:, :, here], p, G[b, p], H[i, p]) * scale
        p_copy(i).start()

    def relate_own():
        i = lax.rem(a, nh)
        go_partner(a).wait_recv()
        own_partner.wait_recv()
        for p in range(2):
            span = slice(p * hc, (p + 1) * hc)
            KO[i, :, span] = (
                product(NF.at[:, :, here], p, G[a, p], H[i, p])
                + product(NF.at[:, :, there], p, GO[p], HO[p])
            ) * scale

    late = nz - 1

    def is_late(b):
        side = jnp.where(lax.rem(b, 2) == x, 0, 1)
        d = jnp.abs(b // 2 - z) + side
        return (d >= late) | (mid & (side == 1) & (d == late - 1))

    def step(s, c):
        def lift(j, c):
            zz = z + (s - 1) * (2 * j - 1)

            @pl.when((s > 0) & (zz == j * (nz - 1)))
            def _():
                b = 2 * zz + 1 - x
                go_x(b, 1).wait_recv()

                @pl.when((j == 0) & (z < nz - 1))
                def _():
                    go_up(b, 1).start()

                @pl.when((j == 1) & (z > 0))
                def _():
                    go_dn(b, 1).start()

            return c

        def hop(k, c):
            j, p = lax.rem(k, 2), k // 2
            zz = z + s * (2 * j - 1)

            @pl.when((s > 0) & (zz >= 0) & (zz < nz))
            def _():
                b = 2 * zz + x
                go_up(b, p).wait_recv()

                @pl.when((j == 0) & (z < nz - 1))
                def _():
                    go_up(b, p).start()

                @pl.when((j == 1) & (z > 0))
                def _():
                    go_dn(b, p).start()

                @pl.when((p == 0) | jnp.logical_not(is_end(zz)))
                def _():
                    go_x(b, p).start()

            return c

        lax.fori_loop(0, 2, hop, 0)
        lax.fori_loop(0, 2, lift, 0)
        lax.fori_loop(2, 4, hop, 0)

        @pl.when((s == 1) & (m == x) & end)
        def _():
            nb_in(NF, z).start()

        @pl.when((s == late - 1) & (m == x) & mid)
        def _():
            i = near(0)
            nb_in(NF, z).start()
            nb_in(NB.at[i], i).wait_recv()
            nb_in(NB.at[i], i).start()

        @pl.when((s == late) & (m == x) & mid)
        def _():
            nb_x(NF, z).start()
            nb_x(NB.at[near(0)], near(0)).start()
            for i in (near(nz - 1), nz - 1 - z):
                nb_in(NB.at[i], i).wait_recv()
                nb_out(NB.at[i], i).start()
            nb_out(NF, z).start()

        def use(k, c):
            j, side = lax.rem(k, 2), k // 2
            d = s - side
            zz = z + d * (2 * j - 1)

            @pl.when((d >= 0) & (zz >= 0) & (zz < nz) & ((d > 0) | (j == 0)))
            def _():
                b = 2 * zz + x + side * (1 - 2 * x)

                @pl.when(side == 1)
                def _():
                    go_x(b, 0).wait_recv()

                    @pl.when(jnp.logical_not(is_end(zz)))
                    def _():
                        go_x(b, 1).wait_recv()

                @pl.when(b // nh == o)
                def _():
                    go_partner(b).start()

                inv_copy(b).wait()
                first, second = G[b, 0], G[b, 1]
                width = 256 if cols % 256 == 0 else 128
                for t in range(0, cols, width):
                    ACC[:, t : t + width] += jnp.dot(
                        first, INV[b, :hc, t : t + width], preferred_element_type=F32
                    ) + jnp.dot(second, INV[b, hc:, t : t + width], preferred_element_type=F32)

                @pl.when(s == 0)
                def _():
                    n_f.wait_recv()

                    @pl.when(b // nh == m)
                    def _():
                        relate_own()

                @pl.when((b // nh == m) & (s > 0) & jnp.logical_not(is_late(b)))
                def _():
                    relate(lax.rem(b, nh))

            return c

        lax.fori_loop(0, 4, use, 0)

        return c

    lax.fori_loop(0, nz + 1, step, 0)

    def l_y(c):
        return remote(LF.at[c, m, here], LF.at[c, m, here], l_send.at[0, c], l_recv.at[0, c], g=1 - y)

    def l_p(c):
        return remote(LF.at[c, m, here], LF.at[c, m, here], l_send.at[1, c], l_recv.at[1, c], mk=o)

    def l_f(c):
        return remote(LF.at[c, m, there], LF.at[c, m, there], l_send.at[2, c], l_recv.at[2, c], mk=o)

    def m_z(c):
        return remote(LF.at[c, m, here], LM.at[c, m, here], m_send.at[3, c], m_recv.at[3, c], an=across)

    def m_y(c):
        return remote(LM.at[c, m, here], LM.at[c, m, here], m_send.at[0, c], m_recv.at[0, c], g=1 - y)

    def m_p(c):
        return remote(LM.at[c, m, here], LM.at[c, m, here], m_send.at[1, c], m_recv.at[1, c], mk=o)

    def m_f(c):
        return remote(LM.at[c, m, there], LM.at[c, m, there], m_send.at[2, c], m_recv.at[2, c], mk=o)

    def e_h(c):
        return remote(
            LF.at[c, m, here], LM.at[c, m, here], m_send.at[0, c], m_recv.at[2 * m, c], an=beside, mk=x
        )

    def e_t(c):
        return remote(
            LF.at[c, m, there], LM.at[c, m, there], m_send.at[1, c], m_recv.at[2 * m + 1, c], an=beside, mk=x
        )

    for c in range(nc):
        LF[c, m, here, :] = ACC[:, c * cw : (c + 1) * cw].astype(BF16)

        @pl.when(mid)
        def _():
            m_z(c).start()

        l_y(c).start()

        @pl.when(mid | (m != x))
        def _():
            l_p(c).start()

        if c < 1:

            @pl.when(end)
            def _():
                e_h(c).start()

    def pass_on(zz):
        @pl.when(end & (m == x) & (zz != z))
        def _():
            nb_c(zz).wait_recv()
            nb_c(zz).start()

    def arrive(zz):
        @pl.when((end | (m == x)) & (zz == z))
        def _():
            nb_local.wait()

        @pl.when((m != x) & (mid | (zz != z)))
        def _():
            nb_c(zz).wait_recv()

    def window(b, c):
        return pl.ds(pl.multiple_of(lax.rem(b, nh) * cols + c * cw, cw), cw)

    def r_copy(c, slot, zz, b):
        return remote(
            R.at[c, slot], reg_out.at[:, window(b, c)], r_send.at[c, slot], r_recv.at[c, lax.rem(b, nh)],
            an=2 * zz + jnp.where(mid, m, x), mk=b // nh,
        )

    def r_local(c, slot, b):
        return pltpu.make_async_copy(R.at[c, slot], reg_out.at[:, window(b, c)], r_loc.at[c])

    keep = (end | (m == x)) & (a // nh == m)
    keep_across = mid & (m == x) & (across // nh == m)

    def score(c, slot, zz, b, ref, stays):
        R[c, slot] = (
            (
                jnp.dot(NB[zz, 0], ref[c, 0], preferred_element_type=F32)
                + jnp.dot(NB[zz, 1], ref[c, 1], preferred_element_type=F32)
            )
            * scale
        ).astype(BF16)

        @pl.when((zz == z) & stays)
        def _():
            r_local(c, slot, b).start()

        @pl.when((zz != z) | jnp.logical_not(stays))
        def _():
            r_copy(c, slot, zz, b).start()

    def rest(i, c):
        @pl.when(is_late(m * nh + i))
        def _():
            relate(i)

        return c

    @pl.when(end)
    def _():
        lax.fori_loop(0, nh, rest, 0)

    def chunk(c, carry):
        @pl.when(c < nc)
        def _():
            l_y(c).wait_recv()

            @pl.when(mid | (m != x))
            def _():
                l_f(c).start()

            @pl.when(end)
            def _():
                e_t(c).start()

                @pl.when(c + 1 < nc)
                def _():
                    e_h(c + 1).start()

            @pl.when(mid)
            def _():
                m_z(c).wait_recv()
                m_y(c).start()
                m_p(c).start()

            @pl.when(c == 0)
            def _():
                pass_on(near(nz - 1))

        @pl.when(c > 0)
        def _():
            e = c - 1

            def regress(ref, i, carry):
                zz = near(jnp.where(mid, i, nz - 1 - i))

                @pl.when(e == 0)
                def _():
                    @pl.when(i != 0)
                    def _():
                        pass_on(zz)

                    arrive(zz)

                score(e, zz, zz, block, ref, keep)
                return carry

            @pl.when(mid | (m == x))
            def _():
                l_p(e).wait_recv()
                l_f(e).wait_recv()
                lax.fori_loop(0, jnp.where(mid, nz // 2, nz), functools.partial(regress, LF), 0)

            @pl.when(end & (m != x))
            def _():
                def part(k, carry):
                    at = pl.ds(pl.multiple_of((y + lax.rem(k, 2) * (1 - 2 * y)) * q, q), q)
                    remote(
                        LM.at[e, k // 2, at], LM.at[e, k // 2, at], m_send.at[0, e], m_recv.at[k, e], mk=o
                    ).wait_recv()
                    return carry

                lax.fori_loop(0, 4, part, 0)
                lax.fori_loop(0, nz, functools.partial(regress, LM), 0)

        return carry

    lax.fori_loop(0, nc + 1, chunk, 0)

    @pl.when(mid)
    def _():
        def chunk_across(c, carry):
            @pl.when(c < nc)
            def _():
                m_y(c).wait_recv()
                m_f(c).start()

            @pl.when(c > 0)
            def _():
                e = c - 1
                m_p(e).wait_recv()
                m_f(e).wait_recv()

                def regress(i, carry):
                    zz = near(i)
                    score(e, nz - 1 - zz, zz, across, LM, keep_across)
                    return carry

                lax.fori_loop(0, nz // 2, regress, 0)

            return carry

        lax.fori_loop(0, nc + 1, chunk_across, 0)
        lax.fori_loop(0, nh, rest, 0)

    n_y.wait_send()
    n_f.wait_send()

    @pl.when(a // nh == o)
    def _():
        own_partner.wait_send()

    for i in range(nh):
        span = slice(i * cols, (i + 1) * cols)

        @pl.when(m * nh + i == a)
        def _():
            kin_out[:, span] = KO[i].astype(BF16)

        @pl.when(m * nh + i != a)
        def _():
            p_copy(i).wait_recv()
            kin_out[:, span] = (KO[i] + PR[i].astype(F32)).astype(BF16)

    def l_sends(c, carry):
        l_y(c).wait_send()

        @pl.when(mid | (m != x))
        def _():
            l_p(c).wait_send()
            l_f(c).wait_send()

        @pl.when(end)
        def _():
            e_h(c).wait_send()
            e_t(c).wait_send()

        @pl.when(mid)
        def _():
            m_z(c).wait_send()
            m_y(c).wait_send()
            m_p(c).wait_send()
            m_f(c).wait_send()

        return carry

    lax.fori_loop(0, nc, l_sends, 0)

    def p_sends(i, c):
        @pl.when(m * nh + i != a)
        def _():
            p_copy(i).wait_send()

        return c

    lax.fori_loop(0, nh, p_sends, 0)

    def g_sends(b, c):
        zz = b // 2
        same = lax.rem(b, 2) == x

        for p in range(2):
            lone = is_end(zz) if p == 1 else False

            @pl.when(same & ((zz == z) | jnp.logical_not(lone)))
            def _():
                go_x(b, p).wait_send()

            @pl.when((same | (lone & (zz == 0))) & (zz <= z) & (z < nz - 1))
            def _():
                go_up(b, p).wait_send()

            @pl.when((same | (lone & (zz == nz - 1))) & (zz >= z) & (z > 0))
            def _():
                go_dn(b, p).wait_send()

        @pl.when(b // nh == o)
        def _():
            go_partner(b).wait_send()

        return c

    lax.fori_loop(0, n, g_sends, 0)

    @pl.when(m == x)
    def _():
        nb_in(NF, z).wait_send()

        @pl.when(mid)
        def _():
            nb_in(NF, near(0)).wait_send()
            nb_x(NF, z).wait_send()
            nb_x(NF, near(0)).wait_send()
            for i in (z, nz - 1 - z, near(nz - 1)):
                nb_out(NF, i).wait_send()

        @pl.when(end)
        def _():
            for i in range(1, nz):
                nb_c(near(i)).wait_send()

    def r_all(c, carry):
        @pl.when(keep | keep_across)
        def _():
            r_local(c, 0, a).wait()

        def r_sends(i, carry):
            own = (i == z) & keep
            other = (i == nz - 1 - z) & keep_across

            @pl.when(jnp.logical_not(own | other))
            def _():
                r_copy(c, i, i, a).wait_send()

            return carry

        lax.fori_loop(0, nz, r_sends, 0)

        def r_recvs(i, carry):
            b = m * nh + i
            own = (b == block) & keep
            other = (b == across) & keep_across

            @pl.when(jnp.logical_not(own | other))
            def _():
                remote(
                    R.at[c, 0], reg_out.at[:, window(i, c)], r_send.at[c, 0], r_recv.at[c, i], mk=o
                ).wait_recv()

            return carry

        lax.fori_loop(0, nh, r_recvs, 0)
        return carry

    lax.fori_loop(0, nc, r_all, 0)


def store_kernel(kin_ref, reg_ref, kin_out, reg_out, sem):
    rows = kin_ref.shape[0] // 4
    copies = [
        pltpu.make_async_copy(src.at[pl.ds(k * rows, rows)], dst.at[pl.ds(k * rows, rows)], sem.at[i, k])
        for i, (src, dst) in enumerate(((kin_ref, kin_out), (reg_ref, reg_out)))
        for k in range(4)
    ]
    for copy in copies:
        copy.start()
    for copy in copies:
        copy.wait()


def kernel_body(n, markers, noncore_geno, noncore_codes, core_geno, core_codes, breed_freqs, core_inverse):
    half = core_geno.shape[1]
    q = half // 2
    cols = core_inverse.shape[1]
    rows = noncore_geno.shape[0]
    nh = nz = n // 2
    nc = 4 if cols % 512 == 0 else 1
    cw = cols // nc
    vmem = pl.BlockSpec(memory_space=pltpu.VMEM)
    anyspace = pl.BlockSpec(memory_space=pl.ANY)
    hbm = pl.BlockSpec(memory_space=pltpu.HBM)
    D = pltpu.SemaphoreType.DMA
    out = jax.ShapeDtypeStruct((rows, nh * cols), BF16)
    held = pltpu.VMEM((rows, nh * cols), BF16)
    related, scores = pl.pallas_call(
        functools.partial(kernel, n, nc, 1.0 / markers),
        out_shape=(held, held),
        in_specs=[hbm] * 6,
        out_specs=(vmem, vmem),
        scratch_shapes=[
            pltpu.VMEM((cols, half), jnp.int32),
            pltpu.VMEM(core_codes.shape, jnp.int32),
            pltpu.VMEM(breed_freqs.shape, F32),
            pltpu.VMEM(noncore_geno.shape, jnp.int32),
            pltpu.VMEM(noncore_codes.shape, jnp.int32),
            pltpu.VMEM((128, half), F32),
            pltpu.VMEM((128, rows), F32),
            pltpu.VMEM((n, 2, q, cols // 2), BF16),
            pltpu.VMEM((nh, 2, q, cols // 2), BF16),
            pltpu.VMEM((2, q, cols // 2), BF16),
            pltpu.VMEM((2, q, cols // 2), BF16),
            pltpu.VMEM((n, cols, cols), BF16),
            pltpu.VMEM((q, cols), F32),
            pltpu.VMEM((2, rows, half), BF16),
            pltpu.VMEM((2, rows, q), BF16),
            pltpu.VMEM((nz, 2, rows, half), BF16),
            pltpu.VMEM((nc, 2, half, cw), BF16),
            pltpu.VMEM((nc, 2, half, cw), BF16),
            pltpu.VMEM((nh, rows, cols), BF16),
            pltpu.VMEM((nh, rows, cols), BF16),
            pltpu.VMEM((nh, rows, cols), F32),
            pltpu.VMEM((nc, nz, rows, cw), BF16),
            D((2,)), D((4,)), D((n,)), D((n, 2)), D((n, 2)), D((n, 2)), D((n, 2)), D((nh,)), D((nh,)), D, D,
            D((3,)), D((3,)), D, D((2, nz)), D((nz,)), D((nz,)), D((3, nc)), D((3, nc)),
            D((4, nc)), D((4, nc)),
            D((nh,)), D((nh,)), D((nc, nz)), D((nc, nh)), D((nc,)),
        ],
        compiler_params=pltpu.CompilerParams(
            collective_id=0, has_side_effects=True, vmem_limit_bytes=54 * 1024 * 1024
        ),
    )(core_geno, core_codes, breed_freqs, noncore_geno, noncore_codes, core_inverse)
    return pl.pallas_call(
        store_kernel,
        out_shape=(out, out),
        in_specs=[vmem] * 2,
        out_specs=(anyspace, anyspace),
        scratch_shapes=[D((2, 4))],
    )(*(pltpu.with_memory_space_constraint(v, pltpu.VMEM) for v in (related, scores)))


def solution(mesh):
    in_specs = (
        P(("grp", "anim"), "mark"),
        P(None, ("grp", "anim")),
        P("anim", "mark"),
        P(None, "anim"),
        P(None, "mark"),
        P(None, "anim"),
    )
    out_specs = (P(("grp", "anim"), "mark"), P(("grp", "anim"), "mark"))
    n = mesh.shape["anim"]

    def body(*args):
        half, cols, rows = args[2].shape[1], args[5].shape[1], args[0].shape[0]
        markers = half * mesh.shape["mark"]
        fits = (
            mesh.shape["grp"] == 2 and mesh.shape["mark"] == 2 and n == 8
            and half % 256 == 0 and cols % 256 == 0 and rows % 128 == 0 and args[4].shape[0] <= 128
            and args[2].shape[0] == cols and n * cols * cols * 2 <= 24 * 2**20
        )
        if fits:
            return kernel_body(n, markers, *args)
        return plain_body(markers, *args)

    return jax.shard_map(body, mesh=mesh, in_specs=in_specs, out_specs=out_specs, check_vma=False)
```

```python
import functools

import jax
import jax.numpy as jnp
from jax import lax
from jax.experimental import pallas as pl
from jax.experimental.pallas import tpu as pltpu
from jax.sharding import PartitionSpec as P

MESH = pl.DeviceIdType.MESH
F32 = jnp.float32
BF16 = jnp.bfloat16


def centre_value(genotypes, breed_codes, breed_freqs):
    fractions = breed_codes.astype(F32) / 32.0
    expected = lax.dot_general(
        fractions, breed_freqs, (((0,), (0,)), ((), ())), precision=lax.Precision.HIGHEST
    )
    return (genotypes.astype(F32) - 2.0 * expected).astype(BF16)


def plain_body(markers, noncore_geno, noncore_codes, core_geno, core_codes, breed_freqs, core_inverse):
    noncore_z = centre_value(noncore_geno, noncore_codes, breed_freqs)
    core_z = centre_value(core_geno, core_codes, breed_freqs)
    rows = lax.all_gather(core_z, "anim", axis=0, tiled=True)
    related = (
        lax.dot_general(noncore_z, rows, (((1,), (1,)), ((), ())), preferred_element_type=F32) / markers
    )
    loading = lax.dot_general(rows, core_inverse, (((0,), (0,)), ((), ())), preferred_element_type=F32)
    scores = (
        jnp.dot(
            noncore_z,
            lax.all_gather(loading.astype(BF16), "anim", axis=1, tiled=True),
            preferred_element_type=F32,
        )
        / markers
    )
    return tuple(
        lax.psum_scatter(v.astype(BF16), "mark", scatter_dimension=1, tiled=True) for v in (related, scores)
    )


def kernel(
    n, nc, scale, geno_hbm, codes_hbm, freqs_hbm, ngeno_hbm, ncodes_hbm, inv_hbm, kin_out, reg_out,
    RAW, codes, freqs, ngeno, ncodes, TF, TC, G, H, GO, HO, INV, ACC, NF, NO, NB, LF, LM, PO, PR, KO, R,
    raw_sem, in_sem, inv_sem, g_recv, up_send, dn_send, x_send, h_send, h_recv, ho_send, ho_recv,
    n_send, n_recv, nb_loc, nb_zsend, nb_xsend, nb_recv, l_send, l_recv, m_send, m_recv,
    p_send, p_recv, r_send, r_recv, r_loc,
):
    nz, nh = n // 2, n // 2
    y, a, m = lax.axis_index("grp"), lax.axis_index("anim"), lax.axis_index("mark")
    z, x = a // 2, lax.rem(a, 2)
    o = 1 - m
    q, hc = G.shape[2:]
    cols = 2 * hc
    breeds = freqs.shape[0]
    cw = cols // nc
    here = pl.ds(pl.multiple_of(y * q, q), q)
    there = pl.ds(pl.multiple_of((1 - y) * q, q), q)
    low = z < nz // 2
    mid = (z > 0) & (z < nz - 1)
    end = jnp.logical_not(mid)
    across = 2 * (nz - 1 - z) + x
    beside = a + 1 - 2 * x
    block = jnp.where(end & (m != x), beside, a)

    def is_end(zz):
        return (zz == 0) | (zz == nz - 1)

    def remote(src, dst, ss, rs, g=None, an=None, mk=None):
        return pltpu.make_async_remote_copy(
            src_ref=src, dst_ref=dst, send_sem=ss, recv_sem=rs,
            device_id=(y if g is None else g, a if an is None else an, m if mk is None else mk),
            device_id_type=MESH,
        )

    barrier = pltpu.get_barrier_semaphore()

    def greet(g=None, an=None, mk=None):
        pl.semaphore_signal(
            barrier, inc=1,
            device_id=(y if g is None else g, a if an is None else an, m if mk is None else mk),
            device_id_type=MESH,
        )

    greet(mk=o)
    greet(an=a + 1 - 2 * x)
    greet(g=1 - y)

    @pl.when(z < nz - 1)
    def _():
        greet(an=a + 2)

    @pl.when(z > 0)
    def _():
        greet(an=a - 2)

    def inv_copy(b):
        return pltpu.make_async_copy(inv_hbm.at[pl.ds(b * cols, cols)], INV.at[b], inv_sem.at[b])

    raw = [
        pltpu.make_async_copy(geno_hbm.at[pl.ds(p * hc, hc)], RAW.at[pl.ds(p * hc, hc)], raw_sem.at[p])
        for p in range(2)
    ]
    small = [
        pltpu.make_async_copy(src, dst, in_sem.at[i])
        for i, (src, dst) in enumerate(
            ((codes_hbm, codes), (freqs_hbm, freqs), (ngeno_hbm, ngeno), (ncodes_hbm, ncodes))
        )
    ]
    for copy in raw + small:
        copy.start()

    lax.fori_loop(0, n, lambda i, c: (inv_copy(lax.rem(a + i, n)).start(), c)[1], 0)

    def go_up(b, p):
        return remote(G.at[b, p], G.at[b, p], up_send.at[b, p], g_recv.at[b, p], an=a + 2)

    def go_dn(b, p):
        return remote(G.at[b, p], G.at[b, p], dn_send.at[b, p], g_recv.at[b, p], an=a - 2)

    def go_x(b, p):
        return remote(G.at[b, p], G.at[b, p], x_send.at[b, p], g_recv.at[b, p], an=a + 1 - 2 * x)

    def go_partner(b):
        i = lax.rem(b, nh)
        return remote(G.at[b], H.at[i], h_send.at[i], h_recv.at[i], mk=o)

    TF[...] = jnp.zeros_like(TF)
    TC[...] = jnp.zeros_like(TC)
    small[0].wait()
    small[1].wait()
    TF[:breeds, :] = freqs[...]

    def centre(p, markers, freq_t, dst):
        for t in range(0, hc, 128):
            at = slice(p * hc + t, p * hc + t + 128)
            expected = freq_t[:, 0:1] * (codes[0:1, at].astype(F32) / 32.0)
            for b in range(1, breeds):
                expected += freq_t[:, b : b + 1] * (codes[b : b + 1, at].astype(F32) / 32.0)
            dst[:, t : t + 128] = (RAW[at, markers].astype(F32).T - 2.0 * expected).astype(BF16)

    freq_t = TF[:, here].T
    for p in range(2):
        raw[p].wait()
        centre(p, here, freq_t, G.at[a, p])
        if p == 0:
            pl.semaphore_wait(barrier, 5 - jnp.where(mid, 0, 1))

        @pl.when(z < nz - 1)
        def _():
            go_up(a, p).start()

        @pl.when(z > 0)
        def _():
            go_dn(a, p).start()

        go_x(a, p).start()

    small[2].wait()
    small[3].wait()
    TC[:breeds, :] = ncodes[...].astype(F32) / 32.0
    code_t = TC[...].T
    expected = code_t[:, 0:1] * freqs[0:1, :]
    for b in range(1, breeds):
        expected += code_t[:, b : b + 1] * freqs[b : b + 1, :]
    NF[m] = (ngeno[...].astype(F32) - 2.0 * expected).astype(BF16)
    npart = remote(NF.at[m], NF.at[m], n_send.at[0], n_recv.at[0], mk=o)
    npart.start()
    n_y = remote(NF.at[m, :, there], NO.at[m], n_send.at[1], n_recv.at[1], g=1 - y)
    n_y.start()
    freq_t = TF[:, there].T
    for p in range(2):
        centre(p, there, freq_t, GO.at[p])
    own_partner = remote(GO, HO, ho_send, ho_recv, mk=o)

    @pl.when(a // nh == o)
    def _():
        own_partner.start()

    ACC[...] = jnp.zeros_like(ACC)
    npart.wait_send()
    remote(NF.at[o], NF.at[o], n_send.at[0], n_recv.at[0], mk=o).wait_recv()
    n_y.wait_recv()
    n_f = remote(NO.at[m], NO.at[m], n_send.at[2], n_recv.at[2], mk=o)
    n_f.start()

    def near(i):
        return jnp.where(low, i, nz - 1 - i)

    def nb_in(src, i):
        return remote(
            src, NB.at[i], nb_zsend.at[0, i], nb_recv.at[i], an=jnp.where(mid, across, 2 * near(1) + x)
        )

    def nb_out(src, i):
        return remote(src, NB.at[i], nb_zsend.at[1, i], nb_recv.at[i], an=2 * near(0) + x)

    def nb_x(src, i):
        return remote(src, NB.at[i], nb_xsend.at[i], nb_recv.at[i], an=a + 1 - 2 * x)

    nb_local = pltpu.make_async_copy(NF, NB.at[z], nb_loc)

    def nb_c(i):
        return remote(NB.at[i], NB.at[i], nb_xsend.at[i], nb_recv.at[i], mk=o)

    @pl.when(end | (m == x))
    def _():
        nb_local.start()

    def p_copy(i):
        return remote(PO.at[i], PR.at[i], p_send.at[i], p_recv.at[i], g=1 - y)

    def product(ref, p, mine, his):
        return jnp.dot(ref[m], mine, preferred_element_type=F32) + jnp.dot(
            ref[o], his, preferred_element_type=F32
        )

    def relate(i):
        b = m * nh + i
        go_partner(b).wait_recv()
        for p in range(2):
            span = slice(p * hc, (p + 1) * hc)
            PO[i, :, span] = (product(NO, p, G[b, p], H[i, p]) * scale).astype(BF16)
            KO[i, :, span] = product(NF.at[:, :, here], p, G[b, p], H[i, p]) * scale
        p_copy(i).start()

    def relate_own():
        i = lax.rem(a, nh)
        go_partner(a).wait_recv()
        own_partner.wait_recv()
        for p in range(2):
            span = slice(p * hc, (p + 1) * hc)
            KO[i, :, span] = (
                product(NF.at[:, :, here], p, G[a, p], H[i, p])
                + product(NF.at[:, :, there], p, GO[p], HO[p])
            ) * scale

    late = nz - 1

    def is_late(b):
        side = jnp.where(lax.rem(b, 2) == x, 0, 1)
        d = jnp.abs(b // 2 - z) + side
        return (d >= late) | (mid & (side == 1) & (d == late - 1))

    def step(s, c):
        def lift(j, c):
            zz = z + (s - 1) * (2 * j - 1)

            @pl.when((s > 0) & (zz == j * (nz - 1)))
            def _():
                b = 2 * zz + 1 - x
                go_x(b, 1).wait_recv()

                @pl.when((j == 0) & (z < nz - 1))
                def _():
                    go_up(b, 1).start()

                @pl.when((j == 1) & (z > 0))
                def _():
                    go_dn(b, 1).start()

            return c

        def hop(k, c):
            j, p = lax.rem(k, 2), k // 2
            zz = z + s * (2 * j - 1)

            @pl.when((s > 0) & (zz >= 0) & (zz < nz))
            def _():
                b = 2 * zz + x
                go_up(b, p).wait_recv()

                @pl.when((j == 0) & (z < nz - 1))
                def _():
                    go_up(b, p).start()

                @pl.when((j == 1) & (z > 0))
                def _():
                    go_dn(b, p).start()

                @pl.when((p == 0) | jnp.logical_not(is_end(zz)))
                def _():
                    go_x(b, p).start()

            return c

        lax.fori_loop(0, 2, hop, 0)
        lax.fori_loop(0, 2, lift, 0)
        lax.fori_loop(2, 4, hop, 0)

        @pl.when((s == 1) & (m == x) & end)
        def _():
            nb_in(NF, z).start()

        @pl.when((s == late - 1) & (m == x) & mid)
        def _():
            i = near(0)
            nb_in(NF, z).start()
            nb_in(NB.at[i], i).wait_recv()
            nb_in(NB.at[i], i).start()

        @pl.when((s == late) & (m == x) & mid)
        def _():
            nb_x(NF, z).start()
            nb_x(NB.at[near(0)], near(0)).start()
            for i in (near(nz - 1), nz - 1 - z):
                nb_in(NB.at[i], i).wait_recv()
                nb_out(NB.at[i], i).start()
            nb_out(NF, z).start()

        def use(k, c):
            j, side = lax.rem(k, 2), k // 2
            d = s - side
            zz = z + d * (2 * j - 1)

            @pl.when((d >= 0) & (zz >= 0) & (zz < nz) & ((d > 0) | (j == 0)))
            def _():
                b = 2 * zz + x + side * (1 - 2 * x)

                @pl.when(side == 1)
                def _():
                    go_x(b, 0).wait_recv()

                    @pl.when(jnp.logical_not(is_end(zz)))
                    def _():
                        go_x(b, 1).wait_recv()

                @pl.when(b // nh == o)
                def _():
                    go_partner(b).start()

                inv_copy(b).wait()
                first, second = G[b, 0], G[b, 1]
                width = 256 if cols % 256 == 0 else 128
                for t in range(0, cols, width):
                    ACC[:, t : t + width] += jnp.dot(
                        first, INV[b, :hc, t : t + width], preferred_element_type=F32
                    ) + jnp.dot(second, INV[b, hc:, t : t + width], preferred_element_type=F32)

                @pl.when(s == 0)
                def _():
                    n_f.wait_recv()

                    @pl.when(b // nh == m)
                    def _():
                        relate_own()

                @pl.when((b // nh == m) & (s > 0) & jnp.logical_not(is_late(b)))
                def _():
                    relate(lax.rem(b, nh))

            return c

        lax.fori_loop(0, 4, use, 0)

        return c

    lax.fori_loop(0, nz + 1, step, 0)

    def l_y(c):
        lone = end & (m != x)
        return remote(
            LF.at[c, m, here], LF.at[c, m, here], l_send.at[0, c], l_recv.at[jnp.where(lone, 2, 0), c],
            g=1 - y, mk=jnp.where(lone, o, m),
        )

    def l_p(c):
        return remote(LF.at[c, m, here], LF.at[c, m, here], l_send.at[1, c], l_recv.at[1, c], mk=o)

    def l_f(c):
        return remote(LF.at[c, m, there], LF.at[c, m, there], l_send.at[2, c], l_recv.at[2, c], mk=o)

    def m_z(c):
        return remote(LF.at[c, m, here], LM.at[c, m, here], m_send.at[3, c], m_recv.at[3, c], an=across)

    def m_y(c):
        return remote(LM.at[c, m, here], LM.at[c, m, here], m_send.at[0, c], m_recv.at[0, c], g=1 - y)

    def m_p(c):
        return remote(LM.at[c, m, here], LM.at[c, m, here], m_send.at[1, c], m_recv.at[1, c], mk=o)

    def m_f(c):
        return remote(LM.at[c, m, there], LM.at[c, m, there], m_send.at[2, c], m_recv.at[2, c], mk=o)

    def e_h(c):
        return remote(
            LF.at[c, m, here], LM.at[c, m, here], m_send.at[0, c], m_recv.at[2 * m, c], an=beside, mk=x
        )

    def e_t(c, k):
        return remote(
            LF.at[c, k, there], LM.at[c, k, there], m_send.at[1 + k, c], m_recv.at[2 * k + 1, c], an=beside, mk=x
        )

    for c in range(nc):
        LF[c, m, here, :] = ACC[:, c * cw : (c + 1) * cw].astype(BF16)

        @pl.when(mid)
        def _():
            m_z(c).start()

        l_y(c).start()

        @pl.when(mid | (m != x))
        def _():
            l_p(c).start()

        @pl.when(end)
        def _():
            e_h(c).start()

    def pass_on(zz):
        @pl.when(end & (m == x) & (zz != z))
        def _():
            nb_c(zz).wait_recv()
            nb_c(zz).start()

    def arrive(zz):
        @pl.when((end | (m == x)) & (zz == z))
        def _():
            nb_local.wait()

        @pl.when((m != x) & (mid | (zz != z)))
        def _():
            nb_c(zz).wait_recv()

    def window(b, c):
        return pl.ds(pl.multiple_of(lax.rem(b, nh) * cols + c * cw, cw), cw)

    def r_copy(c, slot, zz, b):
        return remote(
            R.at[c, slot], reg_out.at[:, window(b, c)], r_send.at[c, slot], r_recv.at[c, lax.rem(b, nh)],
            an=2 * zz + jnp.where(mid, m, x), mk=b // nh,
        )

    def r_local(c, slot, b):
        return pltpu.make_async_copy(R.at[c, slot], reg_out.at[:, window(b, c)], r_loc.at[c])

    keep = (end | (m == x)) & (a // nh == m)
    keep_across = mid & (m == x) & (across // nh == m)

    def score(c, slot, zz, b, ref, stays):
        R[c, slot] = (
            (
                jnp.dot(NB[zz, 0], ref[c, 0], preferred_element_type=F32)
                + jnp.dot(NB[zz, 1], ref[c, 1], preferred_element_type=F32)
            )
            * scale
        ).astype(BF16)

        @pl.when((zz == z) & stays)
        def _():
            r_local(c, slot, b).start()

        @pl.when((zz != z) | jnp.logical_not(stays))
        def _():
            r_copy(c, slot, zz, b).start()

    def rest(i, c):
        @pl.when(is_late(m * nh + i))
        def _():
            relate(i)

        return c

    @pl.when(end)
    def _():
        lax.fori_loop(0, nh, rest, 0)

    def regress(ref, e, i, carry):
        zz = near(jnp.where(mid, i, nz - 1 - i))

        @pl.when(e == 0)
        def _():
            @pl.when(i != 0)
            def _():
                pass_on(zz)

            arrive(zz)

        score(e, zz, zz, block, ref, keep)
        return carry

    def chunk(c, carry):
        @pl.when(c < nc)
        def _():
            @pl.when(mid)
            def _():
                l_y(c).wait_recv()
                l_f(c).start()

            @pl.when(end & (m == x))
            def _():
                l_y(c).wait_recv()
                e_t(c, m).start()
                l_f(c).wait_recv()
                e_t(c, o).start()

            @pl.when(mid)
            def _():
                m_z(c).wait_recv()
                m_y(c).start()
                m_p(c).start()

            @pl.when(c == 0)
            def _():
                pass_on(near(nz - 1))

        @pl.when(c > 0)
        def _():
            e = c - 1

            @pl.when(mid | (m == x))
            def _():
                l_p(e).wait_recv()

                @pl.when(mid)
                def _():
                    l_f(e).wait_recv()

                lax.fori_loop(0, jnp.where(mid, nz // 2, nz), functools.partial(regress, LF, e), 0)

        return carry

    lax.fori_loop(0, nc + 1, chunk, 0)

    @pl.when(end & (m != x))
    def _():
        def part(k, e):
            at = pl.ds(pl.multiple_of((y + lax.rem(k, 2) * (1 - 2 * y)) * q, q), q)
            remote(
                LM.at[e, k // 2, at], LM.at[e, k // 2, at], m_send.at[0, e], m_recv.at[k, e], mk=o
            ).wait_recv()
            return e

        def chunk_beside(e, carry):
            lax.fori_loop(0, 4, part, e)
            lax.fori_loop(0, nz, functools.partial(regress, LM, e), 0)
            return carry

        lax.fori_loop(0, nc, chunk_beside, 0)

    @pl.when(mid)
    def _():
        def chunk_across(c, carry):
            @pl.when(c < nc)
            def _():
                m_y(c).wait_recv()
                m_f(c).start()

            @pl.when(c == 1)
            def _():
                lax.fori_loop(0, nh, rest, 0)

            @pl.when(c > 0)
            def _():
                e = c - 1
                m_p(e).wait_recv()
                m_f(e).wait_recv()

                def regress(i, carry):
                    zz = near(i)
                    score(e, nz - 1 - zz, zz, across, LM, keep_across)
                    return carry

                lax.fori_loop(0, nz // 2, regress, 0)

            return carry

        lax.fori_loop(0, nc + 1, chunk_across, 0)

    n_y.wait_send()
    n_f.wait_send()

    @pl.when(a // nh == o)
    def _():
        own_partner.wait_send()

    for i in range(nh):
        span = slice(i * cols, (i + 1) * cols)

        @pl.when(m * nh + i == a)
        def _():
            kin_out[:, span] = KO[i].astype(BF16)

        @pl.when(m * nh + i != a)
        def _():
            p_copy(i).wait_recv()
            kin_out[:, span] = (KO[i] + PR[i].astype(F32)).astype(BF16)

    def l_sends(c, carry):
        l_y(c).wait_send()

        @pl.when(mid | (m != x))
        def _():
            l_p(c).wait_send()

        @pl.when(mid)
        def _():
            l_f(c).wait_send()

        @pl.when(end)
        def _():
            e_h(c).wait_send()

        @pl.when(end & (m == x))
        def _():
            e_t(c, 0).wait_send()
            e_t(c, 1).wait_send()

        @pl.when(mid)
        def _():
            m_z(c).wait_send()
            m_y(c).wait_send()
            m_p(c).wait_send()
            m_f(c).wait_send()

        return carry

    lax.fori_loop(0, nc, l_sends, 0)

    def p_sends(i, c):
        @pl.when(m * nh + i != a)
        def _():
            p_copy(i).wait_send()

        return c

    lax.fori_loop(0, nh, p_sends, 0)

    def g_sends(b, c):
        zz = b // 2
        same = lax.rem(b, 2) == x

        for p in range(2):
            lone = is_end(zz) if p == 1 else False

            @pl.when(same & ((zz == z) | jnp.logical_not(lone)))
            def _():
                go_x(b, p).wait_send()

            @pl.when((same | (lone & (zz == 0))) & (zz <= z) & (z < nz - 1))
            def _():
                go_up(b, p).wait_send()

            @pl.when((same | (lone & (zz == nz - 1))) & (zz >= z) & (z > 0))
            def _():
                go_dn(b, p).wait_send()

        @pl.when(b // nh == o)
        def _():
            go_partner(b).wait_send()

        return c

    lax.fori_loop(0, n, g_sends, 0)

    @pl.when(m == x)
    def _():
        nb_in(NF, z).wait_send()

        @pl.when(mid)
        def _():
            nb_in(NF, near(0)).wait_send()
            nb_x(NF, z).wait_send()
            nb_x(NF, near(0)).wait_send()
            for i in (z, nz - 1 - z, near(nz - 1)):
                nb_out(NF, i).wait_send()

        @pl.when(end)
        def _():
            for i in range(1, nz):
                nb_c(near(i)).wait_send()

    def r_all(c, carry):
        @pl.when(keep | keep_across)
        def _():
            r_local(c, 0, a).wait()

        def r_sends(i, carry):
            own = (i == z) & keep
            other = (i == nz - 1 - z) & keep_across

            @pl.when(jnp.logical_not(own | other))
            def _():
                r_copy(c, i, i, a).wait_send()

            return carry

        lax.fori_loop(0, nz, r_sends, 0)

        def r_recvs(i, carry):
            b = m * nh + i
            own = (b == block) & keep
            other = (b == across) & keep_across

            @pl.when(jnp.logical_not(own | other))
            def _():
                remote(
                    R.at[c, 0], reg_out.at[:, window(i, c)], r_send.at[c, 0], r_recv.at[c, i], mk=o
                ).wait_recv()

            return carry

        lax.fori_loop(0, nh, r_recvs, 0)
        return carry

    lax.fori_loop(0, nc, r_all, 0)


def store_kernel(kin_ref, reg_ref, kin_out, reg_out, sem):
    rows = kin_ref.shape[0] // 4
    copies = [
        pltpu.make_async_copy(src.at[pl.ds(k * rows, rows)], dst.at[pl.ds(k * rows, rows)], sem.at[i, k])
        for i, (src, dst) in enumerate(((kin_ref, kin_out), (reg_ref, reg_out)))
        for k in range(4)
    ]
    for copy in copies:
        copy.start()
    for copy in copies:
        copy.wait()


def kernel_body(n, markers, noncore_geno, noncore_codes, core_geno, core_codes, breed_freqs, core_inverse):
    half = core_geno.shape[1]
    q = half // 2
    cols = core_inverse.shape[1]
    rows = noncore_geno.shape[0]
    nh = nz = n // 2
    nc = 4 if cols % 512 == 0 else 1
    cw = cols // nc
    vmem = pl.BlockSpec(memory_space=pltpu.VMEM)
    anyspace = pl.BlockSpec(memory_space=pl.ANY)
    hbm = pl.BlockSpec(memory_space=pltpu.HBM)
    D = pltpu.SemaphoreType.DMA
    out = jax.ShapeDtypeStruct((rows, nh * cols), BF16)
    held = pltpu.VMEM((rows, nh * cols), BF16)
    related, scores = pl.pallas_call(
        functools.partial(kernel, n, nc, 1.0 / markers),
        out_shape=(held, held),
        in_specs=[hbm] * 6,
        out_specs=(vmem, vmem),
        scratch_shapes=[
            pltpu.VMEM((cols, half), jnp.int32),
            pltpu.VMEM(core_codes.shape, jnp.int32),
            pltpu.VMEM(breed_freqs.shape, F32),
            pltpu.VMEM(noncore_geno.shape, jnp.int32),
            pltpu.VMEM(noncore_codes.shape, jnp.int32),
            pltpu.VMEM((128, half), F32),
            pltpu.VMEM((128, rows), F32),
            pltpu.VMEM((n, 2, q, cols // 2), BF16),
            pltpu.VMEM((nh, 2, q, cols // 2), BF16),
            pltpu.VMEM((2, q, cols // 2), BF16),
            pltpu.VMEM((2, q, cols // 2), BF16),
            pltpu.VMEM((n, cols, cols), BF16),
            pltpu.VMEM((q, cols), F32),
            pltpu.VMEM((2, rows, half), BF16),
            pltpu.VMEM((2, rows, q), BF16),
            pltpu.VMEM((nz, 2, rows, half), BF16),
            pltpu.VMEM((nc, 2, half, cw), BF16),
            pltpu.VMEM((nc, 2, half, cw), BF16),
            pltpu.VMEM((nh, rows, cols), BF16),
            pltpu.VMEM((nh, rows, cols), BF16),
            pltpu.VMEM((nh, rows, cols), F32),
            pltpu.VMEM((nc, nz, rows, cw), BF16),
            D((2,)), D((4,)), D((n,)), D((n, 2)), D((n, 2)), D((n, 2)), D((n, 2)), D((nh,)), D((nh,)), D, D,
            D((3,)), D((3,)), D, D((2, nz)), D((nz,)), D((nz,)), D((3, nc)), D((3, nc)),
            D((4, nc)), D((4, nc)),
            D((nh,)), D((nh,)), D((nc, nz)), D((nc, nh)), D((nc,)),
        ],
        compiler_params=pltpu.CompilerParams(
            collective_id=0, has_side_effects=True, vmem_limit_bytes=54 * 1024 * 1024
        ),
    )(core_geno, core_codes, breed_freqs, noncore_geno, noncore_codes, core_inverse)
    return pl.pallas_call(
        store_kernel,
        out_shape=(out, out),
        in_specs=[vmem] * 2,
        out_specs=(anyspace, anyspace),
        scratch_shapes=[D((2, 4))],
    )(*(pltpu.with_memory_space_constraint(v, pltpu.VMEM) for v in (related, scores)))


def solution(mesh):
    in_specs = (
        P(("grp", "anim"), "mark"),
        P(None, ("grp", "anim")),
        P("anim", "mark"),
        P(None, "anim"),
        P(None, "mark"),
        P(None, "anim"),
    )
    out_specs = (P(("grp", "anim"), "mark"), P(("grp", "anim"), "mark"))
    n = mesh.shape["anim"]

    def body(*args):
        half, cols, rows = args[2].shape[1], args[5].shape[1], args[0].shape[0]
        markers = half * mesh.shape["mark"]
        fits = (
            mesh.shape["grp"] == 2 and mesh.shape["mark"] == 2 and n == 8
            and half % 256 == 0 and cols % 256 == 0 and rows % 128 == 0 and args[4].shape[0] <= 128
            and args[2].shape[0] == cols and n * cols * cols * 2 <= 24 * 2**20
        )
        if fits:
            return kernel_body(n, markers, *args)
        return plain_body(markers, *args)

    return jax.shard_map(body, mesh=mesh, in_specs=in_specs, out_specs=out_specs, check_vma=False)
```

```python
import functools

import jax
import jax.numpy as jnp
from jax import lax
from jax.experimental import pallas as pl
from jax.experimental.pallas import tpu as pltpu
from jax.sharding import PartitionSpec as P

MESH = pl.DeviceIdType.MESH
F32 = jnp.float32
BF16 = jnp.bfloat16


def centre_value(genotypes, breed_codes, breed_freqs):
    fractions = breed_codes.astype(F32) / 32.0
    expected = lax.dot_general(
        fractions, breed_freqs, (((0,), (0,)), ((), ())), precision=lax.Precision.HIGHEST
    )
    return (genotypes.astype(F32) - 2.0 * expected).astype(BF16)


def plain_body(markers, noncore_geno, noncore_codes, core_geno, core_codes, breed_freqs, core_inverse):
    noncore_z = centre_value(noncore_geno, noncore_codes, breed_freqs)
    core_z = centre_value(core_geno, core_codes, breed_freqs)
    rows = lax.all_gather(core_z, "anim", axis=0, tiled=True)
    related = (
        lax.dot_general(noncore_z, rows, (((1,), (1,)), ((), ())), preferred_element_type=F32) / markers
    )
    loading = lax.dot_general(rows, core_inverse, (((0,), (0,)), ((), ())), preferred_element_type=F32)
    scores = (
        jnp.dot(
            noncore_z,
            lax.all_gather(loading.astype(BF16), "anim", axis=1, tiled=True),
            preferred_element_type=F32,
        )
        / markers
    )
    return tuple(
        lax.psum_scatter(v.astype(BF16), "mark", scatter_dimension=1, tiled=True) for v in (related, scores)
    )


def kernel(
    n, nc, scale, geno_hbm, codes_hbm, freqs_hbm, ngeno_hbm, ncodes_hbm, inv_hbm, kin_out, reg_out,
    RAW, codes, freqs, ngeno, ncodes, TF, TC, G, H, GO, HO, INV, ACC, NF, NO, NB, LF, LM, PO, PR, KO, R,
    raw_sem, in_sem, inv_sem, g_recv, up_send, dn_send, x_send, h_send, h_recv, ho_send, ho_recv,
    n_send, n_recv, nb_loc, nb_zsend, nb_xsend, nb_recv, l_send, l_recv, m_send, m_recv,
    p_send, p_recv, r_send, r_recv, r_loc,
):
    nz, nh = n // 2, n // 2
    y, a, m = lax.axis_index("grp"), lax.axis_index("anim"), lax.axis_index("mark")
    z, x = a // 2, lax.rem(a, 2)
    o = 1 - m
    q, hc = G.shape[2:]
    cols = 2 * hc
    breeds = freqs.shape[0]
    cw = cols // nc
    here = pl.ds(pl.multiple_of(y * q, q), q)
    there = pl.ds(pl.multiple_of((1 - y) * q, q), q)
    low = z < nz // 2
    mid = (z > 0) & (z < nz - 1)
    end = jnp.logical_not(mid)
    across = 2 * (nz - 1 - z) + x
    beside = a + 1 - 2 * x
    block = jnp.where(end & (m != x), beside, a)

    def is_end(zz):
        return (zz == 0) | (zz == nz - 1)

    def remote(src, dst, ss, rs, g=None, an=None, mk=None):
        return pltpu.make_async_remote_copy(
            src_ref=src, dst_ref=dst, send_sem=ss, recv_sem=rs,
            device_id=(y if g is None else g, a if an is None else an, m if mk is None else mk),
            device_id_type=MESH,
        )

    barrier = pltpu.get_barrier_semaphore()

    def greet(g=None, an=None, mk=None):
        pl.semaphore_signal(
            barrier, inc=1,
            device_id=(y if g is None else g, a if an is None else an, m if mk is None else mk),
            device_id_type=MESH,
        )

    greet(mk=o)
    greet(an=a + 1 - 2 * x)
    greet(g=1 - y)

    @pl.when(z < nz - 1)
    def _():
        greet(an=a + 2)

    @pl.when(z > 0)
    def _():
        greet(an=a - 2)

    def inv_copy(b):
        return pltpu.make_async_copy(inv_hbm.at[pl.ds(b * cols, cols)], INV.at[b], inv_sem.at[b])

    raw = [
        pltpu.make_async_copy(geno_hbm.at[pl.ds(p * hc, hc)], RAW.at[pl.ds(p * hc, hc)], raw_sem.at[p])
        for p in range(2)
    ]
    small = [
        pltpu.make_async_copy(src, dst, in_sem.at[i])
        for i, (src, dst) in enumerate(
            ((codes_hbm, codes), (freqs_hbm, freqs), (ngeno_hbm, ngeno), (ncodes_hbm, ncodes))
        )
    ]
    for copy in raw + small:
        copy.start()

    lax.fori_loop(0, n, lambda i, c: (inv_copy(lax.rem(a + i, n)).start(), c)[1], 0)

    def go_up(b, p):
        return remote(G.at[b, p], G.at[b, p], up_send.at[b, p], g_recv.at[b, p], an=a + 2)

    def go_dn(b, p):
        return remote(G.at[b, p], G.at[b, p], dn_send.at[b, p], g_recv.at[b, p], an=a - 2)

    def go_x(b, p):
        return remote(G.at[b, p], G.at[b, p], x_send.at[b, p], g_recv.at[b, p], an=a + 1 - 2 * x)

    def go_partner(b):
        i = lax.rem(b, nh)
        return remote(G.at[b], H.at[i], h_send.at[i], h_recv.at[i], mk=o)

    TF[...] = jnp.zeros_like(TF)
    TC[...] = jnp.zeros_like(TC)
    small[0].wait()
    small[1].wait()
    TF[:breeds, :] = freqs[...]

    def centre(p, markers, freq_t, dst):
        for t in range(0, hc, 128):
            at = slice(p * hc + t, p * hc + t + 128)
            expected = freq_t[:, 0:1] * (codes[0:1, at].astype(F32) / 32.0)
            for b in range(1, breeds):
                expected += freq_t[:, b : b + 1] * (codes[b : b + 1, at].astype(F32) / 32.0)
            dst[:, t : t + 128] = (RAW[at, markers].astype(F32).T - 2.0 * expected).astype(BF16)

    freq_t = TF[:, here].T
    for p in range(2):
        raw[p].wait()
        centre(p, here, freq_t, G.at[a, p])
        if p == 0:
            pl.semaphore_wait(barrier, 5 - jnp.where(mid, 0, 1))

        @pl.when(z < nz - 1)
        def _():
            go_up(a, p).start()

        @pl.when(z > 0)
        def _():
            go_dn(a, p).start()

        go_x(a, p).start()

    small[2].wait()
    small[3].wait()
    TC[:breeds, :] = ncodes[...].astype(F32) / 32.0
    code_t = TC[...].T
    expected = code_t[:, 0:1] * freqs[0:1, :]
    for b in range(1, breeds):
        expected += code_t[:, b : b + 1] * freqs[b : b + 1, :]
    NF[m] = (ngeno[...].astype(F32) - 2.0 * expected).astype(BF16)
    npart = remote(NF.at[m], NF.at[m], n_send.at[0], n_recv.at[0], mk=o)
    npart.start()
    n_y = remote(NF.at[m, :, there], NO.at[m], n_send.at[1], n_recv.at[1], g=1 - y)
    n_y.start()
    freq_t = TF[:, there].T
    for p in range(2):
        centre(p, there, freq_t, GO.at[p])
    own_partner = remote(GO, HO, ho_send, ho_recv, mk=o)

    @pl.when(a // nh == o)
    def _():
        own_partner.start()

    ACC[...] = jnp.zeros_like(ACC)
    npart.wait_send()
    remote(NF.at[o], NF.at[o], n_send.at[0], n_recv.at[0], mk=o).wait_recv()
    n_y.wait_recv()
    n_f = remote(NO.at[m], NO.at[m], n_send.at[2], n_recv.at[2], mk=o)
    n_f.start()

    def near(i):
        return jnp.where(low, i, nz - 1 - i)

    def nb_in(src, i):
        return remote(
            src, NB.at[i], nb_zsend.at[0, i], nb_recv.at[i], an=jnp.where(mid, across, 2 * near(1) + x)
        )

    def nb_out(src, i):
        return remote(src, NB.at[i], nb_zsend.at[1, i], nb_recv.at[i], an=2 * near(0) + x)

    def nb_x(src, i):
        return remote(src, NB.at[i], nb_xsend.at[i], nb_recv.at[i], an=a + 1 - 2 * x)

    nb_local = pltpu.make_async_copy(NF, NB.at[z], nb_loc)

    def nb_c(i):
        return remote(NB.at[i], NB.at[i], nb_xsend.at[i], nb_recv.at[i], mk=o)

    @pl.when(end | (m == x))
    def _():
        nb_local.start()

    def p_copy(i):
        return remote(PO.at[i], PR.at[i], p_send.at[i], p_recv.at[i], g=1 - y)

    def product(ref, p, mine, his):
        return jnp.dot(ref[m], mine, preferred_element_type=F32) + jnp.dot(
            ref[o], his, preferred_element_type=F32
        )

    def relate(i):
        b = m * nh + i
        go_partner(b).wait_recv()
        for p in range(2):
            span = slice(p * hc, (p + 1) * hc)
            PO[i, :, span] = (product(NO, p, G[b, p], H[i, p]) * scale).astype(BF16)
            KO[i, :, span] = product(NF.at[:, :, here], p, G[b, p], H[i, p]) * scale
        p_copy(i).start()

    def relate_own():
        i = lax.rem(a, nh)
        go_partner(a).wait_recv()
        own_partner.wait_recv()
        for p in range(2):
            span = slice(p * hc, (p + 1) * hc)
            KO[i, :, span] = (
                product(NF.at[:, :, here], p, G[a, p], H[i, p])
                + product(NF.at[:, :, there], p, GO[p], HO[p])
            ) * scale

    late = nz - 1

    def is_late(b):
        side = jnp.where(lax.rem(b, 2) == x, 0, 1)
        d = jnp.abs(b // 2 - z) + side
        return (d >= late) | (mid & (side == 1) & (d == late - 1))

    def step(s, c):
        def lift(j, c):
            zz = z + (s - 1) * (2 * j - 1)

            @pl.when((s > 0) & (zz == j * (nz - 1)))
            def _():
                b = 2 * zz + 1 - x
                go_x(b, 1).wait_recv()

                @pl.when((j == 0) & (z < nz - 1))
                def _():
                    go_up(b, 1).start()

                @pl.when((j == 1) & (z > 0))
                def _():
                    go_dn(b, 1).start()

            return c

        def hop(k, c):
            j, p = lax.rem(k, 2), k // 2
            zz = z + s * (2 * j - 1)

            @pl.when((s > 0) & (zz >= 0) & (zz < nz))
            def _():
                b = 2 * zz + x
                go_up(b, p).wait_recv()

                @pl.when((j == 0) & (z < nz - 1))
                def _():
                    go_up(b, p).start()

                @pl.when((j == 1) & (z > 0))
                def _():
                    go_dn(b, p).start()

                @pl.when((p == 0) | jnp.logical_not(is_end(zz)))
                def _():
                    go_x(b, p).start()

            return c

        lax.fori_loop(0, 2, hop, 0)
        lax.fori_loop(0, 2, lift, 0)
        lax.fori_loop(2, 4, hop, 0)

        @pl.when((s == 1) & (m == x) & end)
        def _():
            nb_in(NF, z).start()

        @pl.when((s == late - 1) & (m == x) & mid)
        def _():
            i = near(0)
            nb_in(NF, z).start()
            nb_in(NB.at[i], i).wait_recv()
            nb_in(NB.at[i], i).start()

        @pl.when((s == late) & (m == x) & mid)
        def _():
            nb_x(NF, z).start()
            nb_x(NB.at[near(0)], near(0)).start()
            for i in (near(nz - 1), nz - 1 - z):
                nb_in(NB.at[i], i).wait_recv()
                nb_out(NB.at[i], i).start()
            nb_out(NF, z).start()

        def use(k, c):
            j, side = lax.rem(k, 2), k // 2
            d = s - side
            zz = z + d * (2 * j - 1)

            @pl.when((d >= 0) & (zz >= 0) & (zz < nz) & ((d > 0) | (j == 0)))
            def _():
                b = 2 * zz + x + side * (1 - 2 * x)

                @pl.when(side == 1)
                def _():
                    go_x(b, 0).wait_recv()

                    @pl.when(jnp.logical_not(is_end(zz)))
                    def _():
                        go_x(b, 1).wait_recv()

                @pl.when(b // nh == o)
                def _():
                    go_partner(b).start()

                inv_copy(b).wait()
                first, second = G[b, 0], G[b, 1]
                width = 256 if cols % 256 == 0 else 128
                for t in range(0, cols, width):
                    ACC[:, t : t + width] += jnp.dot(
                        first, INV[b, :hc, t : t + width], preferred_element_type=F32
                    ) + jnp.dot(second, INV[b, hc:, t : t + width], preferred_element_type=F32)

                @pl.when((b // nh == m) & (s > 0) & jnp.logical_not(is_late(b)))
                def _():
                    relate(lax.rem(b, nh))

            return c

        @pl.when(s == 1)
        def _():
            n_f.wait_recv()

        lax.fori_loop(0, 4, use, 0)

        return c

    lax.fori_loop(0, nz + 1, step, 0)

    def l_y(c):
        return remote(LF.at[c, m, here], LF.at[c, m, here], l_send.at[0, c], l_recv.at[0, c], g=1 - y)

    def l_p(c):
        return remote(LF.at[c, m, here], LF.at[c, m, here], l_send.at[1, c], l_recv.at[1, c], mk=o)

    def l_f(c):
        return remote(LF.at[c, m, there], LF.at[c, m, there], l_send.at[2, c], l_recv.at[2, c], mk=o)

    def m_z(c):
        return remote(LF.at[c, m, here], LM.at[c, m, here], m_send.at[3, c], m_recv.at[3, c], an=across)

    def m_y(c):
        return remote(LM.at[c, m, here], LM.at[c, m, here], m_send.at[0, c], m_recv.at[0, c], g=1 - y)

    def m_p(c):
        return remote(LM.at[c, m, here], LM.at[c, m, here], m_send.at[1, c], m_recv.at[1, c], mk=o)

    def m_f(c):
        return remote(LM.at[c, m, there], LM.at[c, m, there], m_send.at[2, c], m_recv.at[2, c], mk=o)

    def e_h(c):
        return remote(
            LF.at[c, m, here], LM.at[c, m, here], m_send.at[0, c], m_recv.at[2 * m, c], an=beside, mk=x
        )

    def e_t(c):
        return remote(
            LF.at[c, m, there], LM.at[c, m, there], m_send.at[1, c], m_recv.at[2 * m + 1, c], an=beside, mk=x
        )

    for c in range(nc):
        LF[c, m, here, :] = ACC[:, c * cw : (c + 1) * cw].astype(BF16)

        @pl.when(mid)
        def _():
            m_z(c).start()

        l_y(c).start()

        @pl.when(mid | (m != x))
        def _():
            l_p(c).start()

        if c < 1:

            @pl.when(end)
            def _():
                e_h(c).start()

    def pass_on(zz):
        @pl.when(end & (m == x) & (zz != z))
        def _():
            nb_c(zz).wait_recv()
            nb_c(zz).start()

    def arrive(zz):
        @pl.when((end | (m == x)) & (zz == z))
        def _():
            nb_local.wait()

        @pl.when((m != x) & (mid | (zz != z)))
        def _():
            nb_c(zz).wait_recv()

    def window(b, c):
        return pl.ds(pl.multiple_of(lax.rem(b, nh) * cols + c * cw, cw), cw)

    def r_copy(c, slot, zz, b):
        return remote(
            R.at[c, slot], reg_out.at[:, window(b, c)], r_send.at[c, slot], r_recv.at[c, lax.rem(b, nh)],
            an=2 * zz + jnp.where(mid, m, x), mk=b // nh,
        )

    def r_local(c, slot, b):
        return pltpu.make_async_copy(R.at[c, slot], reg_out.at[:, window(b, c)], r_loc.at[c])

    keep = (end | (m == x)) & (a // nh == m)
    keep_across = mid & (m == x) & (across // nh == m)

    def score(c, slot, zz, b, ref, stays):
        R[c, slot] = (
            (
                jnp.dot(NB[zz, 0], ref[c, 0], preferred_element_type=F32)
                + jnp.dot(NB[zz, 1], ref[c, 1], preferred_element_type=F32)
            )
            * scale
        ).astype(BF16)

        @pl.when((zz == z) & stays)
        def _():
            r_local(c, slot, b).start()

        @pl.when((zz != z) | jnp.logical_not(stays))
        def _():
            r_copy(c, slot, zz, b).start()

    def rest(i, c):
        @pl.when(is_late(m * nh + i))
        def _():
            relate(i)

        return c

    @pl.when(end)
    def _():
        lax.fori_loop(0, nh, rest, 0)

    def chunk(c, carry):
        @pl.when(c < nc)
        def _():
            l_y(c).wait_recv()

            @pl.when(mid | (m != x))
            def _():
                l_f(c).start()

            @pl.when(end)
            def _():
                e_t(c).start()

                @pl.when(c + 1 < nc)
                def _():
                    e_h(c + 1).start()

            @pl.when(mid)
            def _():
                m_z(c).wait_recv()
                m_y(c).start()
                m_p(c).start()

            @pl.when(c == 0)
            def _():
                pass_on(near(nz - 1))

        @pl.when(c > 0)
        def _():
            e = c - 1

            def regress(ref, i, carry):
                zz = near(jnp.where(mid, i, nz - 1 - i))

                @pl.when(e == 0)
                def _():
                    @pl.when(i != 0)
                    def _():
                        pass_on(zz)

                    arrive(zz)

                score(e, zz, zz, block, ref, keep)
                return carry

            @pl.when(mid | (m == x))
            def _():
                l_p(e).wait_recv()
                l_f(e).wait_recv()
                lax.fori_loop(0, jnp.where(mid, nz // 2, nz), functools.partial(regress, LF), 0)

            @pl.when(end & (m != x))
            def _():
                def part(k, carry):
                    at = pl.ds(pl.multiple_of((y + lax.rem(k, 2) * (1 - 2 * y)) * q, q), q)
                    remote(
                        LM.at[e, k // 2, at], LM.at[e, k // 2, at], m_send.at[0, e], m_recv.at[k, e], mk=o
                    ).wait_recv()
                    return carry

                lax.fori_loop(0, 4, part, 0)
                lax.fori_loop(0, nz, functools.partial(regress, LM), 0)

        return carry

    lax.fori_loop(0, nc + 1, chunk, 0)

    @pl.when(mid)
    def _():
        def chunk_across(c, carry):
            @pl.when(c < nc)
            def _():
                m_y(c).wait_recv()
                m_f(c).start()

            @pl.when(c > 0)
            def _():
                e = c - 1
                m_p(e).wait_recv()
                m_f(e).wait_recv()

                def regress(i, carry):
                    zz = near(i)
                    score(e, nz - 1 - zz, zz, across, LM, keep_across)
                    return carry

                lax.fori_loop(0, nz // 2, regress, 0)

            return carry

        lax.fori_loop(0, nc + 1, chunk_across, 0)
        lax.fori_loop(0, nh, rest, 0)

    @pl.when(a // nh == m)
    def _():
        relate_own()

    n_y.wait_send()
    n_f.wait_send()

    @pl.when(a // nh == o)
    def _():
        own_partner.wait_send()

    for i in range(nh):
        span = slice(i * cols, (i + 1) * cols)

        @pl.when(m * nh + i == a)
        def _():
            kin_out[:, span] = KO[i].astype(BF16)

        @pl.when(m * nh + i != a)
        def _():
            p_copy(i).wait_recv()
            kin_out[:, span] = (KO[i] + PR[i].astype(F32)).astype(BF16)

    def l_sends(c, carry):
        l_y(c).wait_send()

        @pl.when(mid | (m != x))
        def _():
            l_p(c).wait_send()
            l_f(c).wait_send()

        @pl.when(end)
        def _():
            e_h(c).wait_send()
            e_t(c).wait_send()

        @pl.when(mid)
        def _():
            m_z(c).wait_send()
            m_y(c).wait_send()
            m_p(c).wait_send()
            m_f(c).wait_send()

        return carry

    lax.fori_loop(0, nc, l_sends, 0)

    def p_sends(i, c):
        @pl.when(m * nh + i != a)
        def _():
            p_copy(i).wait_send()

        return c

    lax.fori_loop(0, nh, p_sends, 0)

    def g_sends(b, c):
        zz = b // 2
        same = lax.rem(b, 2) == x

        for p in range(2):
            lone = is_end(zz) if p == 1 else False

            @pl.when(same & ((zz == z) | jnp.logical_not(lone)))
            def _():
                go_x(b, p).wait_send()

            @pl.when((same | (lone & (zz == 0))) & (zz <= z) & (z < nz - 1))
            def _():
                go_up(b, p).wait_send()

            @pl.when((same | (lone & (zz == nz - 1))) & (zz >= z) & (z > 0))
            def _():
                go_dn(b, p).wait_send()

        @pl.when(b // nh == o)
        def _():
            go_partner(b).wait_send()

        return c

    lax.fori_loop(0, n, g_sends, 0)

    @pl.when(m == x)
    def _():
        nb_in(NF, z).wait_send()

        @pl.when(mid)
        def _():
            nb_in(NF, near(0)).wait_send()
            nb_x(NF, z).wait_send()
            nb_x(NF, near(0)).wait_send()
            for i in (z, nz - 1 - z, near(nz - 1)):
                nb_out(NF, i).wait_send()

        @pl.when(end)
        def _():
            for i in range(1, nz):
                nb_c(near(i)).wait_send()

    def r_all(c, carry):
        @pl.when(keep | keep_across)
        def _():
            r_local(c, 0, a).wait()

        def r_sends(i, carry):
            own = (i == z) & keep
            other = (i == nz - 1 - z) & keep_across

            @pl.when(jnp.logical_not(own | other))
            def _():
                r_copy(c, i, i, a).wait_send()

            return carry

        lax.fori_loop(0, nz, r_sends, 0)

        def r_recvs(i, carry):
            b = m * nh + i
            own = (b == block) & keep
            other = (b == across) & keep_across

            @pl.when(jnp.logical_not(own | other))
            def _():
                remote(
                    R.at[c, 0], reg_out.at[:, window(i, c)], r_send.at[c, 0], r_recv.at[c, i], mk=o
                ).wait_recv()

            return carry

        lax.fori_loop(0, nh, r_recvs, 0)
        return carry

    lax.fori_loop(0, nc, r_all, 0)


def store_kernel(kin_ref, reg_ref, kin_out, reg_out, sem):
    rows = kin_ref.shape[0] // 4
    copies = [
        pltpu.make_async_copy(src.at[pl.ds(k * rows, rows)], dst.at[pl.ds(k * rows, rows)], sem.at[i, k])
        for i, (src, dst) in enumerate(((kin_ref, kin_out), (reg_ref, reg_out)))
        for k in range(4)
    ]
    for copy in copies:
        copy.start()
    for copy in copies:
        copy.wait()


def kernel_body(n, markers, noncore_geno, noncore_codes, core_geno, core_codes, breed_freqs, core_inverse):
    half = core_geno.shape[1]
    q = half // 2
    cols = core_inverse.shape[1]
    rows = noncore_geno.shape[0]
    nh = nz = n // 2
    nc = 4 if cols % 512 == 0 else 1
    cw = cols // nc
    vmem = pl.BlockSpec(memory_space=pltpu.VMEM)
    anyspace = pl.BlockSpec(memory_space=pl.ANY)
    hbm = pl.BlockSpec(memory_space=pltpu.HBM)
    D = pltpu.SemaphoreType.DMA
    out = jax.ShapeDtypeStruct((rows, nh * cols), BF16)
    held = pltpu.VMEM((rows, nh * cols), BF16)
    related, scores = pl.pallas_call(
        functools.partial(kernel, n, nc, 1.0 / markers),
        out_shape=(held, held),
        in_specs=[hbm] * 6,
        out_specs=(vmem, vmem),
        scratch_shapes=[
            pltpu.VMEM((cols, half), jnp.int32),
            pltpu.VMEM(core_codes.shape, jnp.int32),
            pltpu.VMEM(breed_freqs.shape, F32),
            pltpu.VMEM(noncore_geno.shape, jnp.int32),
            pltpu.VMEM(noncore_codes.shape, jnp.int32),
            pltpu.VMEM((128, half), F32),
            pltpu.VMEM((128, rows), F32),
            pltpu.VMEM((n, 2, q, cols // 2), BF16),
            pltpu.VMEM((nh, 2, q, cols // 2), BF16),
            pltpu.VMEM((2, q, cols // 2), BF16),
            pltpu.VMEM((2, q, cols // 2), BF16),
            pltpu.VMEM((n, cols, cols), BF16),
            pltpu.VMEM((q, cols), F32),
            pltpu.VMEM((2, rows, half), BF16),
            pltpu.VMEM((2, rows, q), BF16),
            pltpu.VMEM((nz, 2, rows, half), BF16),
            pltpu.VMEM((nc, 2, half, cw), BF16),
            pltpu.VMEM((nc, 2, half, cw), BF16),
            pltpu.VMEM((nh, rows, cols), BF16),
            pltpu.VMEM((nh, rows, cols), BF16),
            pltpu.VMEM((nh, rows, cols), F32),
            pltpu.VMEM((nc, nz, rows, cw), BF16),
            D((2,)), D((4,)), D((n,)), D((n, 2)), D((n, 2)), D((n, 2)), D((n, 2)), D((nh,)), D((nh,)), D, D,
            D((3,)), D((3,)), D, D((2, nz)), D((nz,)), D((nz,)), D((3, nc)), D((3, nc)),
            D((4, nc)), D((4, nc)),
            D((nh,)), D((nh,)), D((nc, nz)), D((nc, nh)), D((nc,)),
        ],
        compiler_params=pltpu.CompilerParams(
            collective_id=0, has_side_effects=True, vmem_limit_bytes=54 * 1024 * 1024
        ),
    )(core_geno, core_codes, breed_freqs, noncore_geno, noncore_codes, core_inverse)
    return pl.pallas_call(
        store_kernel,
        out_shape=(out, out),
        in_specs=[vmem] * 2,
        out_specs=(anyspace, anyspace),
        scratch_shapes=[D((2, 4))],
    )(*(pltpu.with_memory_space_constraint(v, pltpu.VMEM) for v in (related, scores)))


def solution(mesh):
    in_specs = (
        P(("grp", "anim"), "mark"),
        P(None, ("grp", "anim")),
        P("anim", "mark"),
        P(None, "anim"),
        P(None, "mark"),
        P(None, "anim"),
    )
    out_specs = (P(("grp", "anim"), "mark"), P(("grp", "anim"), "mark"))
    n = mesh.shape["anim"]

    def body(*args):
        half, cols, rows = args[2].shape[1], args[5].shape[1], args[0].shape[0]
        markers = half * mesh.shape["mark"]
        fits = (
            mesh.shape["grp"] == 2 and mesh.shape["mark"] == 2 and n == 8
            and half % 256 == 0 and cols % 256 == 0 and rows % 128 == 0 and args[4].shape[0] <= 128
            and args[2].shape[0] == cols and n * cols * cols * 2 <= 24 * 2**20
        )
        if fits:
            return kernel_body(n, markers, *args)
        return plain_body(markers, *args)

    return jax.shard_map(body, mesh=mesh, in_specs=in_specs, out_specs=out_specs, check_vma=False)
```
